128 devices in a mesh: pipe: 16 (over y_lo, z, core), seq: 8 (over x, y_hi).
Axes of the slice: x: 4, y: 4 (y_hi: 2, y_lo: 2; y = y_hi * 2 + y_lo), z: 4, core: 2. Of those that a mesh axis runs over, the one named last changes fastest.
Arguments:
- x_fwd: float32 [16, 1024, 2048], P('pipe', 'seq'), may hold values from -12 to 12
- x_bwd: float32 [16, 1024, 2048], P('pipe', 'seq'), may hold values from -12 to 12
- grad_in: float32 [16, 1024, 2048], P('pipe', 'seq'), may hold values from -6 to 6
- gain: float32 [16, 2048], P('pipe'), may hold values from 0.25 to 1.75
- w_query: bfloat16 [16, 2048, 2048], P('pipe', None, 'seq'), may hold values from -2 to 2
- w_key: bfloat16 [16, 2048, 2048], P('pipe', None, 'seq'), may hold values from -2 to 2
- w_value: bfloat16 [16, 2048, 2048], P('pipe', None, 'seq'), may hold values from -0.125 to 0.125
- w_out: bfloat16 [16, 2048, 2048], P('pipe', None, 'seq'), may hold values from -0.125 to 0.125
Outputs:
- act_next: float32 [16, 1024, 2048], P('pipe', 'seq')
- grad_prev: float32 [16, 1024, 2048], P('pipe', 'seq')
The draws below stay inside these ranges and needn't reach their ends.
All inputs are finite; a program needn't handle non-finite values.
Results may differ from the reference program's by a relative error of at most 0.012.
The reference program's roundings to bfloat16 on the way count: a program that leaves them out, or rounds other values in their place, can miss the bound.
Values may be sent and summed in bfloat16 or wider, within the bound.
A program may use at most 192 MiB of HBM per device.

```python
import math
import jax
import jax.numpy as jnp
from jax import lax

D = 2048
H = 16
HD = 128
HH = 2048
L = 1024
SECTIONS = 16


def query_base(key):
    base = jax.random.normal(jax.random.fold_in(key, 101), (SECTIONS, D, HH), jnp.float32)
    return jnp.clip(base, -6.0, 6.0) / math.sqrt(D)


def draw_w_query(key, part):
    return jnp.clip(3.0 * query_base(key), -2.0, 2.0).astype(jnp.bfloat16)


def draw_w_key(key, part):
    noise = jnp.clip(jax.random.normal(jax.random.fold_in(key, 102), (SECTIONS, D, HH), jnp.float32), -6.0, 6.0) / math.sqrt(D)
    values = noise
    return jnp.clip(values, -2.0, 2.0).astype(jnp.bfloat16)


def activation_draw(key, salt):
    source = jax.random.fold_in(key, salt)
    values = 0.5 * jnp.clip(jax.random.normal(jax.random.fold_in(source, 5), (SECTIONS, L, D), jnp.float32), -6.0, 6.0)
    return jnp.clip(values, -12.0, 12.0)


def draw_x_fwd(key, part):
    return activation_draw(key, 21)


def draw_x_bwd(key, part):
    return activation_draw(key, 22)


def shard_levels(stream_key, dims, split, low, top_value):
    factor_of = 1.0
    for dim, blocks in split:
        heights = jax.random.uniform(jax.random.fold_in(jax.random.fold_in(stream_key, 6), dim), (blocks,), jnp.float32, low / len(split), top_value / len(split))
        factor_of = factor_of * jnp.repeat(jnp.exp(heights), dims[dim] // blocks).reshape((-1,) + (1,) * (len(dims) - 1 - dim))
    return factor_of


def bell_draw(own_key, dims, spread, reach, shards=(), dtype=jnp.bfloat16):
    result = spread * jax.random.normal(own_key, dims, jnp.float32)
    if shards:
        result = result * shard_levels(own_key, dims, shards, -0.22, 0.18)
    return jnp.clip(result, -reach, reach).astype(dtype)


def setup_inputs(seed: int = 0) -> dict:
    seeds = jax.random.split(jax.random.key(seed), 9)
    x_fwd = draw_x_fwd(jax.random.fold_in(seeds[8], 71), 0)
    x_bwd = draw_x_bwd(jax.random.fold_in(seeds[8], 71), 0)
    grad_in = bell_draw(seeds[2], (SECTIONS, L, D), 1.0, 6.0, ((0, 16), (1, 8)), jnp.float32)
    gain = jnp.clip(1.0 + 0.15 * jax.random.normal(seeds[3], (SECTIONS, D), jnp.float32), 0.25, 1.75)
    w_query = draw_w_query(jax.random.fold_in(seeds[8], 71), 0)
    w_key = draw_w_key(jax.random.fold_in(seeds[8], 71), 0)
    w_value = bell_draw(seeds[6], (SECTIONS, D, HH), D ** -0.5, 0.125, ((0, 16), (2, 8)))
    w_out = bell_draw(seeds[7], (SECTIONS, D, HH), HH ** -0.5, 0.125, ((0, 16), (2, 8)))
    return {"x_fwd": x_fwd, "x_bwd": x_bwd, "grad_in": grad_in, "gain": gain, "w_query": w_query, "w_key": w_key, "w_value": w_value, "w_out": w_out}


def rope_tables(positions):
    half_dim = HD // 2
    inverse = 10000.0 ** (-(jnp.arange(half_dim).astype(jnp.float32) * 2.0 / HD))
    angles = positions.astype(jnp.float32)[:, None] * inverse[None, :]
    return (jnp.cos(angles)[:, None, :], jnp.sin(angles)[:, None, :])

def rotate(values, cosine, sine_table):
    shaped = values.reshape(values.shape[0], -1, HD)
    first_half = shaped[..., :HD // 2]
    second_half = shaped[..., HD // 2:]
    output = jnp.concatenate([first_half * cosine - second_half * sine_table, second_half * cosine + first_half * sine_table], -1)
    return output.reshape(values.shape)

def rotate_back(values, cosine, sine_table):
    shaped = values.reshape(values.shape[0], -1, HD)
    first_half = shaped[..., :HD // 2]
    second_half = shaped[..., HD // 2:]
    output = jnp.concatenate([first_half * cosine + second_half * sine_table, second_half * cosine - first_half * sine_table], -1)
    return output.reshape(values.shape)

def normalize(inputs, gain_row):
    inv_rms = lax.rsqrt(lax.optimization_barrier(jnp.mean(inputs * inputs, -1, keepdims=True)) + 1e-05)
    return ((inputs * inv_rms * gain_row).astype(jnp.bfloat16), inv_rms)

def times_t(left, right):
    return lax.dot_general(left, right, (((1,), (1,)), ((), ())), preferred_element_type=jnp.float32)

def per_head(values):
    return values.reshape(values.shape[0], H, HD).transpose(1, 0, 2)

def join_heads(values):
    return values.transpose(1, 0, 2).reshape(values.shape[1], H * HD)

def attend(query, key_rows, value_rows):
    score_scale = HD ** (-0.5)

    def one_head(operands):
        query_h, key_h, value_h = operands
        scores = jnp.dot(query_h, key_h.T, preferred_element_type=jnp.float32) * score_scale
        probs = jax.nn.softmax(scores, axis=-1)
        return jnp.dot(probs.astype(jnp.bfloat16), value_h, preferred_element_type=jnp.float32).astype(jnp.bfloat16)
    return join_heads(lax.map(one_head, (per_head(query), per_head(key_rows), per_head(value_rows))))

def attend_back(query, key_rows, value_rows, grad_out):
    score_scale = HD ** (-0.5)

    def one_head(operands):
        query_h, key_h, value_h, grad_h = operands
        scores = jnp.dot(query_h, key_h.T, preferred_element_type=jnp.float32) * score_scale
        probs = jax.nn.softmax(scores, axis=-1)
        value_grad = jnp.dot(probs.astype(jnp.bfloat16).T, grad_h, preferred_element_type=jnp.float32).astype(jnp.bfloat16)
        prob_grad = jnp.dot(grad_h, value_h.T, preferred_element_type=jnp.float32)
        row_delta = lax.optimization_barrier(jnp.sum(probs * prob_grad, -1, keepdims=True))
        score_grad = (probs * (prob_grad - row_delta) * score_scale).astype(jnp.bfloat16)
        query_grad = jnp.dot(score_grad, key_h, preferred_element_type=jnp.float32)
        key_grad = jnp.dot(score_grad.T, query_h, preferred_element_type=jnp.float32)
        return (query_grad, key_grad, value_grad)
    query_grad, key_grad, value_grad = lax.map(one_head, (per_head(query), per_head(key_rows), per_head(value_rows), per_head(grad_out)))
    return (join_heads(query_grad), join_heads(key_grad), join_heads(value_grad))

def section(operands):
    act_in, saved_in, grad, gain_row, query_w, key_w, value_w, out_w = operands
    length = act_in.shape[0]
    cosine, sine_table = rope_tables(jnp.arange(length).astype(jnp.int32))

    def project(normed):
        query = rotate(jnp.dot(normed, query_w, preferred_element_type=jnp.float32), cosine, sine_table).astype(jnp.bfloat16)
        key_rows = rotate(jnp.dot(normed, key_w, preferred_element_type=jnp.float32), cosine, sine_table).astype(jnp.bfloat16)
        value_rows = jnp.dot(normed, value_w, preferred_element_type=jnp.float32).astype(jnp.bfloat16)
        return (query, key_rows, value_rows)
    normed_fwd, inv_fwd = normalize(act_in, gain_row)
    normed_bwd, inv_bwd = normalize(saved_in, gain_row)
    attn = attend(*project(normed_fwd))
    act_out = act_in + times_t(attn, out_w)
    d_attn = jnp.dot(grad.astype(jnp.bfloat16), out_w, preferred_element_type=jnp.float32).astype(jnp.bfloat16)
    query_b, key_b, value_b = project(normed_bwd)
    query_grad, key_grad, value_grad = attend_back(query_b, key_b, value_b, d_attn)
    query_grad = rotate_back(query_grad, cosine, sine_table).astype(jnp.bfloat16)
    key_grad = rotate_back(key_grad, cosine, sine_table).astype(jnp.bfloat16)
    d_normed = times_t(query_grad, query_w) + times_t(key_grad, key_w) + times_t(value_grad, value_w)
    gain_grad = d_normed * gain_row
    d_input = inv_bwd * gain_grad - saved_in * inv_bwd * inv_bwd * inv_bwd * lax.optimization_barrier(jnp.mean(saved_in * gain_grad, -1, keepdims=True))
    return (act_out, grad + d_input)

def reference(x_fwd, x_bwd, grad_in, gain, w_query, w_key, w_value, w_out):
    act_out, d_input = lax.map(section, (x_fwd, x_bwd, grad_in, gain, w_query, w_key, w_value, w_out))
    return (jnp.roll(act_out, 1, axis=0), jnp.roll(d_input, -1, axis=0))
```

```python
import jax
import jax.numpy as jnp
from jax import lax
from jax.sharding import PartitionSpec as P

HD = 128


def passed_along(value, axis, steps):
    count = lax.axis_size(axis)
    pairs = [(source, (source + steps) % count) for source in range(count)]
    return lax.ppermute(value, axis, pairs)


def rope_tables(positions):
    half_dim = HD // 2
    inverse = 10000.0 ** (-(jnp.arange(half_dim).astype(jnp.float32) * 2.0 / HD))
    angles = positions.astype(jnp.float32)[:, None] * inverse[None, :]
    return (jnp.cos(angles)[:, None, :], jnp.sin(angles)[:, None, :])


def rotate(values, cosine, sine_table):
    shaped = values.reshape(values.shape[0], -1, HD)
    first_half = shaped[..., : HD // 2]
    second_half = shaped[..., HD // 2 :]
    output = jnp.concatenate(
        [
            first_half * cosine - second_half * sine_table,
            second_half * cosine + first_half * sine_table,
        ],
        -1,
    )
    return output.reshape(values.shape)


def rotate_back(values, cosine, sine_table):
    shaped = values.reshape(values.shape[0], -1, HD)
    first_half = shaped[..., : HD // 2]
    second_half = shaped[..., HD // 2 :]
    output = jnp.concatenate(
        [
            first_half * cosine + second_half * sine_table,
            second_half * cosine - first_half * sine_table,
        ],
        -1,
    )
    return output.reshape(values.shape)


def normalize(inputs, gain_row):
    inv_rms = lax.rsqrt(jnp.mean(inputs * inputs, -1, keepdims=True) + 1e-05)
    return ((inputs * inv_rms * gain_row).astype(jnp.bfloat16), inv_rms)


def times_t(left, right):
    return lax.dot_general(
        left, right, (((1,), (1,)), ((), ())), preferred_element_type=jnp.float32
    )


def split_heads(values):
    return values.reshape(values.shape[0], -1, HD)


def attend(query, key_rows, value_rows):
    length = query.shape[0]
    score_scale = HD ** (-0.5)
    key_heads = split_heads(key_rows)
    value_heads = split_heads(value_rows)
    query_blocks = split_heads(query).reshape(length // length, length, -1, HD)

    def one_block(query_block):
        scores = (
            jnp.einsum("qhd,khd->hqk", query_block, key_heads, preferred_element_type=jnp.float32)
            * score_scale
        )
        probs = jax.nn.softmax(scores, axis=-1)
        output = jnp.einsum(
            "hqk,khd->qhd",
            probs.astype(jnp.bfloat16),
            value_heads,
            preferred_element_type=jnp.float32,
        )
        return output.astype(jnp.bfloat16)

    return lax.map(one_block, query_blocks).reshape(length, -1)


def attend_back(query, key_rows, value_rows, grad_out, cosine, sine_table):
    length = query.shape[0]
    score_scale = HD ** (-0.5)
    key_heads = split_heads(key_rows)
    value_heads = split_heads(value_rows)
    query_blocks = split_heads(query).reshape(length // length, length, -1, HD)
    grad_blocks = split_heads(grad_out).reshape(length // length, length, -1, HD)

    def step(totals, operands):
        query_block, grad_block = operands
        scores = (
            jnp.einsum("qhd,khd->hqk", query_block, key_heads, preferred_element_type=jnp.float32)
            * score_scale
        )
        probs = jax.nn.softmax(scores, axis=-1)
        value_grad = jnp.einsum(
            "hqk,qhd->khd",
            probs.astype(jnp.bfloat16),
            grad_block,
            preferred_element_type=jnp.float32,
        )
        prob_grad = jnp.einsum(
            "qhd,khd->hqk", grad_block, value_heads, preferred_element_type=jnp.float32
        )
        row_delta = jnp.sum(probs * prob_grad, -1, keepdims=True)
        score_grad = (probs * (prob_grad - row_delta) * score_scale).astype(jnp.bfloat16)
        query_grad = jnp.einsum(
            "hqk,khd->qhd", score_grad, key_heads, preferred_element_type=jnp.float32
        )
        key_grad = jnp.einsum(
            "hqk,qhd->khd", score_grad, query_block, preferred_element_type=jnp.float32
        )
        return ((totals[0] + key_grad, totals[1] + value_grad), query_grad)

    zero_heads = jnp.zeros(key_heads.shape, jnp.float32)
    (key_total, value_total), query_grads = lax.scan(
        step, (zero_heads, zero_heads), (query_blocks, grad_blocks)
    )
    query_grad = rotate_back(query_grads.reshape(length, -1), cosine, sine_table).astype(
        jnp.bfloat16
    )
    key_grad = rotate_back(key_total.reshape(length, -1), cosine, sine_table).astype(jnp.bfloat16)
    return (query_grad, key_grad, value_total.reshape(length, -1).astype(jnp.bfloat16))


def shards(x_fwd, x_bwd, grad_in, gain, w_query, w_key, w_value, w_out):
    act_in = x_fwd[0]
    saved_in = x_bwd[0]
    grad = grad_in[0]
    gain_row = gain[0]
    local_rows = act_in.shape[0]
    length = local_rows * lax.axis_size("seq")
    normed_fwd, inv_fwd = normalize(act_in, gain_row)
    normed_bwd, inv_bwd = normalize(saved_in, gain_row)
    grad_low = grad.astype(jnp.bfloat16)
    full_cos, full_sin = rope_tables(jnp.arange(length))
    all_fwd = lax.all_gather(normed_fwd, "seq", axis=0, tiled=True)
    all_bwd = lax.all_gather(normed_bwd, "seq", axis=0, tiled=True)
    all_grad = lax.all_gather(grad_low, "seq", axis=0, tiled=True)

    def project(normed):
        query = rotate(
            jnp.dot(normed, w_query[0], preferred_element_type=jnp.float32), full_cos, full_sin
        ).astype(jnp.bfloat16)
        key_rows = rotate(
            jnp.dot(normed, w_key[0], preferred_element_type=jnp.float32), full_cos, full_sin
        ).astype(jnp.bfloat16)
        value_rows = jnp.dot(normed, w_value[0], preferred_element_type=jnp.float32).astype(
            jnp.bfloat16
        )
        return (query, key_rows, value_rows)

    attn = attend(*project(all_fwd))
    branch = lax.psum_scatter(
        times_t(attn, w_out[0]).astype(jnp.bfloat16), "seq", scatter_dimension=0, tiled=True
    )
    attn_grad = jnp.dot(all_grad, w_out[0], preferred_element_type=jnp.float32).astype(jnp.bfloat16)
    query_b, key_b, value_b = project(all_bwd)
    query_grad, key_grad, value_grad = attend_back(
        query_b, key_b, value_b, attn_grad, full_cos, full_sin
    )
    d_normed = lax.psum_scatter(
        (
            times_t(query_grad, w_query[0])
            + times_t(key_grad, w_key[0])
            + times_t(value_grad, w_value[0])
        ).astype(jnp.bfloat16),
        "seq",
        scatter_dimension=0,
        tiled=True,
    ).astype(jnp.float32)
    act_out = act_in + branch.astype(jnp.float32)
    gain_grad = d_normed * gain_row
    d_input = inv_bwd * gain_grad - saved_in * inv_bwd * inv_bwd * inv_bwd * jnp.mean(
        saved_in * gain_grad, -1, keepdims=True
    )
    sent_forward = passed_along(act_out.astype(jnp.bfloat16), "pipe", 1).astype(act_out.dtype)
    sent_backward = passed_along((grad + d_input).astype(jnp.bfloat16), "pipe", -1).astype(
        jnp.float32
    )
    return (sent_forward[None], sent_backward[None])


def solution(mesh):
    placed = (
        P("pipe", "seq", None),
        P("pipe", "seq", None),
        P("pipe", "seq", None),
        P("pipe", None),
        P("pipe", None, "seq"),
        P("pipe", None, "seq"),
        P("pipe", None, "seq"),
        P("pipe", None, "seq"),
    )
    return jax.shard_map(
        shards,
        mesh=mesh,
        in_specs=placed,
        out_specs=(P("pipe", "seq", None), P("pipe", "seq", None)),
        check_vma=False,
    )
```

```python
import math

import jax
import jax.numpy as jnp
import numpy as np
from jax import lax
from jax.experimental import pallas as pl
from jax.experimental.pallas import tpu as pltpu
from jax.sharding import PartitionSpec as P

HD = 128
MESH = pl.DeviceIdType.MESH
F32 = jnp.float32
BF16 = jnp.bfloat16
SCALE = HD ** (-0.5)
LOG2E = math.log2(math.e)


def rope_constants(length):
    inverse = 10000.0 ** (-(np.arange(HD // 2, dtype=np.float64) * 2.0 / HD))
    angles = np.arange(length, dtype=np.float64)[:, None] * inverse[None, :]
    cosine, sine = np.cos(angles), np.sin(angles)
    return (
        np.concatenate([cosine, cosine], 1).astype(np.float32),
        np.concatenate([-sine, sine], 1).astype(np.float32),
    )


def dot_nn(left, right):
    return jnp.dot(left, right, preferred_element_type=F32)


def dot_nt(left, right):
    return lax.dot_general(left, right, (((1,), (1,)), ((), ())), preferred_element_type=F32)


def kernel(
    x_fwd_hbm,
    x_bwd_hbm,
    grad_hbm,
    gain_ref,
    wq_hbm,
    wk_hbm,
    wv_hbm,
    wo_hbm,
    cos_hbm,
    sin_hbm,
    act_ref,
    dgrad_ref,
    x_fwd,
    x_bwd,
    grad,
    wq,
    wk,
    wv,
    wo,
    cos,
    sin,
    w3t,
    wot,
    gat_f,
    gat_b,
    gat_g,
    q_ref,
    k_ref,
    v_ref,
    g_ref,
    kt_ref,
    vt_ref,
    dk_acc,
    dv_acc,
    dqkv,
    attn,
    part_b,
    part_f,
    recv_b,
    recv_f,
    out_b,
    out_f,
    load_sem,
    send_sem,
    recv_sem,
):
    rows = x_fwd.shape[0]
    half, quarter = rows // 2, rows // 4
    length, width = gat_f.shape
    feats = wq.shape[1]
    heads = feats // HD
    pipe, seq = lax.axis_index("pipe"), lax.axis_index("seq")
    n_pipe = lax.axis_size("pipe")
    n_x = lax.axis_size("seq") // 2
    my_x, my_y = lax.div(seq, 2), lax.rem(seq, 2)
    left_x, right_x, far_x = (lax.rem(my_x + step, n_x) for step in (n_x - 1, 1, 2))
    own_row, other_row = my_y, 1 - my_y

    def slot(x, y):
        return x * 2 + y

    def at(x, y, start, count):
        return pl.ds(pl.multiple_of(slot(x, y) * rows + start, 32), count)

    devices = {
        "L": (pipe, slot(left_x, my_y)),
        "R": (pipe, slot(right_x, my_y)),
        "Y": (pipe, slot(my_x, 1 - my_y)),
        "N": (lax.rem(pipe + 1, n_pipe), seq),
        "P": (lax.rem(pipe + n_pipe - 1, n_pipe), seq),
    }

    loads = {}

    def load(index, src, dst):
        loads[index] = pltpu.make_async_copy(src, dst, load_sem.at[index])
        loads[index].start()

    load(0, x_bwd_hbm, x_bwd)
    load(1, grad_hbm, grad)
    load(2, x_fwd_hbm, x_fwd)
    load(3, wq_hbm, wq)
    load(4, wk_hbm, wk)
    load(5, wv_hbm, wv)
    load(6, wo_hbm, wo)
    load(7, cos_hbm, cos)
    load(8, sin_hbm, sin)

    barrier = pltpu.get_barrier_semaphore()
    for device in devices.values():
        pl.semaphore_signal(barrier, inc=1, device_id=device, device_id_type=MESH)

    copies = {}

    def describe(name):
        index, refs, where = copies[name]
        src, dst = refs()
        return pltpu.make_async_remote_copy(
            src_ref=src,
            dst_ref=dst,
            send_sem=send_sem.at[index],
            recv_sem=recv_sem.at[index],
            device_id=devices[where],
            device_id_type=MESH,
        )

    def send(name, refs, where):
        copies[name] = (len(copies), refs, where)
        describe(name).start()

    def arrived(name):
        describe(name).wait_recv()

    def normalize_into(source, target):
        def body(i, carry):
            here = pl.ds(pl.multiple_of(i * quarter, quarter), quarter)
            values = source[here, :]
            inv_rms = lax.rsqrt(jnp.mean(values * values, -1, keepdims=True) + 1e-05)
            there = at(my_x, my_y, i * quarter, quarter)
            target[there, :] = (values * inv_rms * gain_ref[...]).astype(BF16)
            return carry

        lax.fori_loop(0, rows // quarter, body, 0)

    def round_into(source, target):
        def body(i, carry):
            here = pl.ds(pl.multiple_of(i * quarter, quarter), quarter)
            target[at(my_x, my_y, i * quarter, quarter), :] = source[here, :].astype(BF16)
            return carry

        lax.fori_loop(0, rows // quarter, body, 0)

    def pass_on(tag, buf, x, y, start, count, where):
        send(tag + where, lambda: (buf.at[at(x, y, start, count)],) * 2, where)

    def gather_start(tag, buf):
        pass_on(tag + "a0", buf, my_x, my_y, 0, half, "Y")
        for where in "LR":
            pass_on(tag + "a0", buf, my_x, my_y, 0, half, where)
        for where in "LRY":
            pass_on(tag + "b0", buf, my_x, my_y, half, half, where)

    def gather_near_a(tag, buf):
        arrived(tag + "a0R")
        pass_on(tag + "a1", buf, left_x, my_y, 0, quarter, "R")
        arrived(tag + "a0L")
        pass_on(tag + "a1", buf, right_x, my_y, quarter, quarter, "L")

    def gather_cross_a(tag, buf):
        arrived(tag + "a0Y")
        for where in "LR":
            pass_on(tag + "a2", buf, my_x, other_row, 0, half, where)

    def gather_near_b(tag, buf):
        arrived(tag + "b0R")
        pass_on(tag + "b1", buf, left_x, my_y, half, quarter, "R")
        pass_on(tag + "b1l", buf, left_x, my_y, half, half, "Y")
        arrived(tag + "b0L")
        pass_on(tag + "b1", buf, right_x, my_y, half + quarter, quarter, "L")
        pass_on(tag + "b1r", buf, right_x, my_y, half, half, "Y")

    def gather_far_b(tag, buf):
        arrived(tag + "b1R")
        pass_on(tag + "b2r", buf, far_x, my_y, half, quarter, "Y")
        arrived(tag + "b1L")
        pass_on(tag + "b2l", buf, far_x, my_y, half + quarter, quarter, "Y")

    def gather_far_a(tag, buf):
        arrived(tag + "a2R")
        pass_on(tag + "a3", buf, left_x, other_row, 0, quarter, "R")
        arrived(tag + "a2L")
        pass_on(tag + "a3", buf, right_x, other_row, quarter, quarter, "L")

    def gather_end(tag, buf):
        for name in ("a1R", "a1L", "b0Y", "b1lY", "b1rY", "a3R", "a3L", "b2rY", "b2lY"):
            arrived(tag + name)

    places = {}
    cursor = 0
    for name, count in (
        ("a0R0", quarter),
        ("a0L0", quarter),
        ("a0R1", quarter),
        ("a0L1", quarter),
        ("a1R0", half),
        ("a1L0", half),
        ("a1R1", half),
        ("a1L1", half),
        ("a2Y", half),
        ("b0Yf", half),
        ("b0Yr", half),
        ("b0Yl", half),
        ("b0Ym", half),
        ("b1R", quarter),
        ("b1L", quarter),
        ("b2R", half),
        ("b2L", half),
    ):
        places[name] = pl.ds(cursor, count)
        cursor += count

    def to(tag, name, part, recv, x, y, start, count, where):
        send(
            tag + name, lambda: (part.at[at(x, y, start, count)], recv.at[places[name]]), where
        )

    def add_in(part, recv, name, x, y, start, count):
        here = at(x, y, start, count)
        part[here, :] = (part[here, :].astype(F32) + recv[places[name], :].astype(F32)).astype(BF16)

    def reduce_far(tag, part, recv):
        for w, y in ((1, other_row), (0, own_row)):
            to(tag, f"a0R{w}", part, recv, far_x, y, 0, quarter, "R")
            to(tag, f"a0L{w}", part, recv, far_x, y, quarter, quarter, "L")
        to(tag, "b0Yf", part, recv, far_x, other_row, half, half, "Y")

    def reduce_cross(tag, part, recv, x, name):
        to(tag, name, part, recv, x, other_row, half, half, "Y")

    def reduce_near_a(tag, part, recv):
        for w, y in ((1, other_row), (0, own_row)):
            arrived(tag + f"a0R{w}")
            add_in(part, recv, f"a0R{w}", right_x, y, 0, quarter)
            to(tag, f"a1R{w}", part, recv, right_x, y, 0, half, "R")
            arrived(tag + f"a0L{w}")
            add_in(part, recv, f"a0L{w}", left_x, y, quarter, quarter)
            to(tag, f"a1L{w}", part, recv, left_x, y, 0, half, "L")

    def reduce_far_b(tag, part, recv):
        arrived(tag + "b0Yf")
        add_in(part, recv, "b0Yf", far_x, own_row, half, half)
        to(tag, "b1R", part, recv, far_x, own_row, half, quarter, "R")
        to(tag, "b1L", part, recv, far_x, own_row, half + quarter, quarter, "L")
        arrived(tag + "b0Yr")
        add_in(part, recv, "b0Yr", right_x, own_row, half, half)
        arrived(tag + "b0Yl")
        add_in(part, recv, "b0Yl", left_x, own_row, half, half)

    def reduce_cross_a(tag, part, recv):
        arrived(tag + "a1R1")
        arrived(tag + "a1L1")
        add_in(part, recv, "a1R1", my_x, other_row, 0, half)
        add_in(part, recv, "a1L1", my_x, other_row, 0, half)
        to(tag, "a2Y", part, recv, my_x, other_row, 0, half, "Y")

    def reduce_near_b(tag, part, recv):
        arrived(tag + "b1R")
        add_in(part, recv, "b1R", right_x, own_row, half, quarter)
        to(tag, "b2R", part, recv, right_x, own_row, half, half, "R")
        arrived(tag + "b1L")
        add_in(part, recv, "b1L", left_x, own_row, half + quarter, quarter)
        to(tag, "b2L", part, recv, left_x, own_row, half, half, "L")

    def last_a(tag):
        for name in ("a1R0", "a1L0", "a2Y"):
            arrived(tag + name)
        return ("a1R0", "a1L0", "a2Y")

    def last_b(tag):
        for name in ("b2R", "b2L", "b0Ym"):
            arrived(tag + name)
        return ("b2R", "b2L", "b0Ym")

    step_rows = 16

    def total_of(part, recv, names, start, i):
        offset = pl.multiple_of(i * step_rows, step_rows)
        here = pl.ds(pl.multiple_of(slot(my_x, my_y) * rows + start + offset, step_rows), step_rows)
        total = part[here, :].astype(F32)
        for name in names:
            total += recv[pl.ds(places[name].start + offset, step_rows), :].astype(F32)
        return total

    def finish_act(part, recv, names, start, name):
        def body(i, carry):
            here = pl.ds(start + pl.multiple_of(i * step_rows, step_rows), step_rows)
            out_f[here, :] = (x_fwd[here, :] + total_of(part, recv, names, start, i)).astype(BF16)
            return carry

        lax.fori_loop(0, half // step_rows, body, 0)
        send(name, lambda: (out_f.at[pl.ds(start, half)], act_ref.at[pl.ds(start, half)]), "N")

    def finish_grad(part, recv, names, start, name):
        def body(i, carry):
            here = pl.ds(start + pl.multiple_of(i * step_rows, step_rows), step_rows)
            saved = x_bwd[here, :]
            inv_rms = lax.rsqrt(jnp.mean(saved * saved, -1, keepdims=True) + 1e-05)
            gain_grad = total_of(part, recv, names, start, i) * gain_ref[...]
            mean = jnp.mean(saved * gain_grad, -1, keepdims=True)
            d_input = inv_rms * gain_grad - saved * (inv_rms * inv_rms * inv_rms * mean)
            out_b[here, :] = (grad[here, :] + d_input).astype(BF16)
            return carry

        lax.fori_loop(0, half // step_rows, body, 0)
        send(name, lambda: (out_b.at[pl.ds(start, half)], dgrad_ref.at[pl.ds(start, half)]), "P")

    block = 256
    blocks = length // block

    def rotated(values, here, sign):
        out = values * cos[here, :]
        turned = pltpu.roll(values, HD // 2, 1) * sin[here, :]
        return out + turned if sign > 0 else out - turned

    def project(buf):
        def body(i, carry):
            here = pl.ds(pl.multiple_of(i * block, block), block)
            normed = buf[here, :]
            query = dot_nn(normed, wq[...])
            key = dot_nn(normed, wk[...])
            for h in range(heads):
                head = slice(h * HD, (h + 1) * HD)
                q_ref[here, head] = rotated(query[:, head], here, 1).astype(BF16)
                turned = rotated(key[:, head], here, 1)
                k_ref[here, head] = turned.astype(BF16)
                kt_ref[head, here] = turned.T.astype(BF16)
            value = dot_nn(normed, wv[...])
            v_ref[here, :] = value.astype(BF16)
            vt_ref[:, here] = value.T.astype(BF16)
            return carry

        lax.fori_loop(0, blocks, body, 0)

    def project_grad(buf):
        def body(i, carry):
            here = pl.ds(pl.multiple_of(i * block, block), block)
            g_ref[here, :] = dot_nn(buf[here, :], wo[...]).astype(BF16)
            return carry

        lax.fori_loop(0, blocks, body, 0)

    def run_actions(actions, h, i):
        for number, todo in actions.items():
            if number // blocks == h:

                @pl.when(i == number % blocks)
                def _(todo=todo):
                    for act in todo:
                        act()

    def exponentials(h, here):
        head = slice(h * HD, (h + 1) * HD)
        scores = dot_nt(k_ref[:, head], q_ref[here, head])
        top = jnp.max(scores, axis=0, keepdims=True)
        weights = jnp.exp2((scores - top) * (SCALE * LOG2E))
        return weights, 1.0 / jnp.sum(weights, axis=0, keepdims=True)

    def attend_back(actions):
        for h in range(heads):
            head = slice(h * HD, (h + 1) * HD)
            dk_acc[...] = jnp.zeros_like(dk_acc)
            dv_acc[...] = jnp.zeros_like(dv_acc)

            def body(i, carry, h=h, head=head):
                run_actions(actions, h, i)
                here = pl.ds(pl.multiple_of(i * block, block), block)
                weights, inverse = exponentials(h, here)
                probs = weights * inverse
                d_out = g_ref[here, head]
                dv_acc[...] += dot_nn(probs.astype(BF16), d_out)
                d_probs = dot_nt(v_ref[:, head], d_out)
                delta = jnp.sum(probs * d_probs, axis=0, keepdims=True)
                d_scores = (probs * (d_probs - delta) * SCALE).astype(BF16)
                dk_acc[...] += dot_nn(d_scores, q_ref[here, head])
                d_query = dot_nn(kt_ref[head, :], d_scores).T
                dqkv[here, head] = rotated(d_query, here, -1).astype(BF16)
                return carry

            lax.fori_loop(0, blocks, body, 0)

            def close(i, carry, h=h):
                here = pl.ds(pl.multiple_of(i * block, block), block)
                d_key = rotated(dk_acc[here, :], here, -1)
                dqkv[here, feats + h * HD : feats + (h + 1) * HD] = d_key.astype(BF16)
                dqkv[here, 2 * feats + h * HD : 2 * feats + (h + 1) * HD] = dv_acc[here, :].astype(BF16)
                return carry

            lax.fori_loop(0, blocks, close, 0)

    def attend(actions):
        for h in range(heads):
            head = slice(h * HD, (h + 1) * HD)

            def body(i, carry, h=h, head=head):
                run_actions(actions, h, i)
                here = pl.ds(pl.multiple_of(i * block, block), block)
                weights, inverse = exponentials(h, here)
                out = dot_nn(vt_ref[head, :], weights.astype(BF16)) * inverse
                attn[here, head] = out.T.astype(BF16)
                return carry

            lax.fori_loop(0, blocks, body, 0)

    columns = 512

    def multiply_out(source, weights, part, x):
        here = pl.ds(pl.multiple_of(x * block, block), block)

        def body(i, carry):
            there = pl.ds(pl.multiple_of(i * columns, columns), columns)
            part[here, there] = dot_nn(source[here, :], weights[:, there]).astype(BF16)
            return carry

        lax.fori_loop(0, width // columns, body, 0)

    def transpose_into(source, target, offset):
        def body(i, carry):
            here = pl.ds(pl.multiple_of(i * feats, feats), feats)
            target[offset : offset + feats, here] = source[here, :].T
            return carry

        lax.fori_loop(0, width // feats, body, 0)

    loads[0].wait()
    normalize_into(x_bwd, gat_b)
    pl.semaphore_wait(barrier, len(devices))
    gather_start("B", gat_b)
    loads[1].wait()
    round_into(grad, gat_g)
    loads[2].wait()
    normalize_into(x_fwd, gat_f)
    gather_near_a("B", gat_b)
    gather_cross_a("B", gat_b)
    for index in range(3, 9):
        loads[index].wait()
    gather_start("G", gat_g)
    transpose_into(wq, w3t, 0)
    gather_near_b("B", gat_b)
    gather_far_b("B", gat_b)
    transpose_into(wk, w3t, feats)
    gather_far_a("B", gat_b)
    transpose_into(wv, w3t, 2 * feats)
    transpose_into(wo, wot, 0)
    gather_near_a("G", gat_g)
    gather_cross_a("G", gat_g)
    gather_near_b("G", gat_g)
    gather_far_b("G", gat_g)
    gather_start("F", gat_f)
    gather_end("B", gat_b)
    project(gat_b)
    gather_far_a("G", gat_g)
    gather_end("G", gat_g)
    project_grad(gat_g)
    attend_back(
        {
            0: [lambda: gather_near_a("F", gat_f)],
            1: [lambda: gather_cross_a("F", gat_f)],
            3: [lambda: gather_near_b("F", gat_f)],
            4: [lambda: gather_far_b("F", gat_f)],
            6: [lambda: gather_far_a("F", gat_f)],
        }
    )
    gather_end("F", gat_f)

    multiply_out(dqkv, w3t, part_b, far_x)
    reduce_far("RB", part_b, recv_b)
    multiply_out(dqkv, w3t, part_b, right_x)
    reduce_cross("RB", part_b, recv_b, right_x, "b0Yr")
    multiply_out(dqkv, w3t, part_b, left_x)
    reduce_cross("RB", part_b, recv_b, left_x, "b0Yl")
    multiply_out(dqkv, w3t, part_b, my_x)
    reduce_cross("RB", part_b, recv_b, my_x, "b0Ym")
    reduce_near_a("RB", part_b, recv_b)
    project(gat_f)
    reduce_far_b("RB", part_b, recv_b)
    attend(
        {
            2: [lambda: reduce_cross_a("RB", part_b, recv_b)],
            4: [lambda: reduce_near_b("RB", part_b, recv_b)],
        }
    )

    multiply_out(attn, wot, part_f, far_x)
    reduce_far("RF", part_f, recv_f)
    multiply_out(attn, wot, part_f, right_x)
    reduce_cross("RF", part_f, recv_f, right_x, "b0Yr")
    multiply_out(attn, wot, part_f, left_x)
    reduce_cross("RF", part_f, recv_f, left_x, "b0Yl")
    multiply_out(attn, wot, part_f, my_x)
    reduce_cross("RF", part_f, recv_f, my_x, "b0Ym")
    finish_grad(part_b, recv_b, last_a("RB"), 0, "PBa")
    reduce_near_a("RF", part_f, recv_f)
    finish_grad(part_b, recv_b, last_b("RB"), half, "PBb")
    reduce_far_b("RF", part_f, recv_f)
    reduce_cross_a("RF", part_f, recv_f)
    reduce_near_b("RF", part_f, recv_f)
    finish_act(part_f, recv_f, last_a("RF"), 0, "PFa")
    finish_act(part_f, recv_f, last_b("RF"), half, "PFb")
    for name in ("PBa", "PBb", "PFa", "PFb"):
        arrived(name)
    for name in copies:
        describe(name).wait_send()


def shards(x_fwd, x_bwd, grad_in, gain, w_query, w_key, w_value, w_out):
    rows, width = x_fwd.shape[1:]
    feats = w_query.shape[2]
    length = rows * lax.axis_size("seq")
    cosine, sine = (jnp.asarray(table) for table in rope_constants(length))
    anywhere = pl.BlockSpec(memory_space=pl.ANY)
    vmem = pltpu.VMEM
    recv_rows = rows * 7
    n_copies = 96
    act, dgrad = pl.pallas_call(
        kernel,
        out_shape=[jax.ShapeDtypeStruct((rows, width), BF16)] * 2,
        in_specs=[anywhere] * 3 + [pl.BlockSpec(memory_space=pltpu.VMEM)] + [anywhere] * 6,
        out_specs=[anywhere] * 2,
        scratch_shapes=[vmem((rows, width), F32)] * 3
        + [vmem((width, feats), BF16)] * 4
        + [vmem((length, HD), F32)] * 2
        + [vmem((3 * feats, width), BF16), vmem((feats, width), BF16)]
        + [vmem((length, width), BF16)] * 3
        + [vmem((length, feats), BF16)] * 4
        + [vmem((feats, length), BF16)] * 2
        + [vmem((length, HD), F32)] * 2
        + [vmem((length, 3 * feats), BF16), vmem((length, feats), BF16)]
        + [vmem((length, width), BF16)] * 2
        + [vmem((recv_rows, width), BF16)] * 2
        + [vmem((rows, width), BF16)] * 2
        + [
            pltpu.SemaphoreType.DMA((9,)),
            pltpu.SemaphoreType.DMA((n_copies,)),
            pltpu.SemaphoreType.DMA((n_copies,)),
        ],
        compiler_params=pltpu.CompilerParams(
            collective_id=0, has_side_effects=True, vmem_limit_bytes=67_043_328
        ),
        name="relay_attention",
    )(
        x_fwd[0],
        x_bwd[0],
        grad_in[0],
        gain,
        w_query[0],
        w_key[0],
        w_value[0],
        w_out[0],
        cosine,
        sine,
    )
    return (act.astype(F32)[None], dgrad.astype(F32)[None])


def solution(mesh):
    placed = (
        P("pipe", "seq", None),
        P("pipe", "seq", None),
        P("pipe", "seq", None),
        P("pipe", None),
        P("pipe", None, "seq"),
        P("pipe", None, "seq"),
        P("pipe", None, "seq"),
        P("pipe", None, "seq"),
    )
    return jax.shard_map(
        shards,
        mesh=mesh,
        in_specs=placed,
        out_specs=(P("pipe", "seq", None), P("pipe", "seq", None)),
        check_vma=False,
    )
```

```python
import math

import jax
import jax.numpy as jnp
import numpy as np
from jax import lax
from jax.experimental import pallas as pl
from jax.experimental.pallas import tpu as pltpu
from jax.sharding import PartitionSpec as P

HD = 128
MESH = pl.DeviceIdType.MESH
F32 = jnp.float32
BF16 = jnp.bfloat16
SCALE = HD ** (-0.5)
LOG2E = math.log2(math.e)


def rope_constants(length):
    inverse = 10000.0 ** (-(np.arange(HD // 2, dtype=np.float64) * 2.0 / HD))
    angles = np.arange(length, dtype=np.float64)[:, None] * inverse[None, :]
    cosine, sine = np.cos(angles), np.sin(angles)
    return (
        np.concatenate([cosine, cosine], 1).astype(np.float32),
        np.concatenate([-sine, sine], 1).astype(np.float32),
    )


def dot_nn(left, right):
    return jnp.dot(left, right, preferred_element_type=F32)


def dot_nt(left, right):
    return lax.dot_general(left, right, (((1,), (1,)), ((), ())), preferred_element_type=F32)


def kernel(
    x_fwd_hbm,
    x_bwd_hbm,
    grad_hbm,
    gain_ref,
    wq_hbm,
    wk_hbm,
    wv_hbm,
    wo_hbm,
    cos_hbm,
    sin_hbm,
    act_ref,
    dgrad_ref,
    x_fwd,
    x_bwd,
    grad,
    wq,
    wk,
    wv,
    wo,
    wo_y,
    cos,
    sin,
    w3t,
    wot,
    gat_f,
    gat_b,
    gat_g,
    q_ref,
    k_ref,
    v_ref,
    g_ref,
    kt_ref,
    vt_ref,
    dk_acc,
    dv_acc,
    dqkv,
    attn,
    attn_y,
    d_send,
    part_b,
    part_f,
    recv_b,
    recv_f,
    out_b,
    out_f,
    load_sem,
    send_sem,
    recv_sem,
):
    rows = x_fwd.shape[0]
    half, quarter = rows // 2, rows // 4
    length, width = gat_f.shape
    feats = wq.shape[1]
    heads = feats // HD
    pipe, seq = lax.axis_index("pipe"), lax.axis_index("seq")
    n_pipe = lax.axis_size("pipe")
    n_x = lax.axis_size("seq") // 2
    my_x, my_y = lax.div(seq, 2), lax.rem(seq, 2)
    left_x, right_x, far_x = (lax.rem(my_x + step, n_x) for step in (n_x - 1, 1, 2))
    own_row, other_row = my_y, 1 - my_y

    def slot(x, y):
        return x * 2 + y

    def at(x, y, start, count):
        return pl.ds(pl.multiple_of(slot(x, y) * rows + start, 16), count)

    others = {"f": far_x, "r": right_x, "l": left_x, "m": my_x}
    devices = {
        "L": (pipe, slot(left_x, my_y)),
        "R": (pipe, slot(right_x, my_y)),
        "Y": (pipe, slot(my_x, 1 - my_y)),
        "N": (lax.rem(pipe + 1, n_pipe), seq),
        "P": (lax.rem(pipe + n_pipe - 1, n_pipe), seq),
    }

    loads = {}

    def load(index, src, dst):
        loads[index] = pltpu.make_async_copy(src, dst, load_sem.at[index])
        loads[index].start()

    load(0, x_bwd_hbm, x_bwd)
    load(1, grad_hbm, grad)
    load(2, x_fwd_hbm, x_fwd)
    load(3, wq_hbm, wq)
    load(4, wk_hbm, wk)
    load(5, wv_hbm, wv)
    load(6, wo_hbm, wo)
    load(7, cos_hbm, cos)
    load(8, sin_hbm, sin)

    barrier = pltpu.get_barrier_semaphore()
    for device in devices.values():
        pl.semaphore_signal(barrier, inc=1, device_id=device, device_id_type=MESH)

    copies = {}

    def describe(name):
        index, refs, where = copies[name]
        src, dst = refs()
        return pltpu.make_async_remote_copy(
            src_ref=src,
            dst_ref=dst,
            send_sem=send_sem.at[index],
            recv_sem=recv_sem.at[index],
            device_id=devices[where],
            device_id_type=MESH,
        )

    def send(name, refs, where):
        copies[name] = (len(copies), refs, where)
        describe(name).start()

    def arrived(name):
        describe(name).wait_recv()

    def normalize_into(source, target):
        def body(i, carry):
            here = pl.ds(pl.multiple_of(i * quarter, quarter), quarter)
            values = source[here, :]
            inv_rms = lax.rsqrt(jnp.mean(values * values, -1, keepdims=True) + 1e-05)
            there = at(my_x, my_y, i * quarter, quarter)
            target[there, :] = (values * inv_rms * gain_ref[...]).astype(BF16)
            return carry

        lax.fori_loop(0, rows // quarter, body, 0)

    def round_into(source, target):
        def body(i, carry):
            here = pl.ds(pl.multiple_of(i * quarter, quarter), quarter)
            target[in_row(my_x, i * quarter, quarter), :] = source[here, :].astype(BF16)
            return carry

        lax.fori_loop(0, rows // quarter, body, 0)

    def pass_on(tag, buf, x, y, start, count, where):
        send(tag + where, lambda: (buf.at[at(x, y, start, count)],) * 2, where)

    def gather_start(tag, buf, split):
        pass_on(tag + "a0", buf, my_x, my_y, 0, split, "Y")
        for where in "LR":
            pass_on(tag + "a0", buf, my_x, my_y, 0, split, where)
        for where in "LRY":
            pass_on(tag + "b0", buf, my_x, my_y, split, rows - split, where)

    def gather_near_a(tag, buf, split):
        part = split // 2
        arrived(tag + "a0R")
        pass_on(tag + "a1", buf, left_x, my_y, 0, part, "R")
        arrived(tag + "a0L")
        pass_on(tag + "a1", buf, right_x, my_y, part, part, "L")

    def gather_cross_a(tag, buf, split):
        arrived(tag + "a0Y")
        for where in "LR":
            pass_on(tag + "a2", buf, my_x, other_row, 0, split, where)

    def gather_near_b(tag, buf, split):
        count = rows - split
        part = count // 2
        arrived(tag + "b0R")
        pass_on(tag + "b1", buf, left_x, my_y, split, part, "R")
        pass_on(tag + "b1l", buf, left_x, my_y, split, count, "Y")
        arrived(tag + "b0L")
        pass_on(tag + "b1", buf, right_x, my_y, split + part, part, "L")
        pass_on(tag + "b1r", buf, right_x, my_y, split, count, "Y")

    def gather_far_b(tag, buf, split):
        part = (rows - split) // 2
        arrived(tag + "b1R")
        pass_on(tag + "b2r", buf, far_x, my_y, split, part, "Y")
        arrived(tag + "b1L")
        pass_on(tag + "b2l", buf, far_x, my_y, split + part, part, "Y")

    def gather_far_a(tag, buf, split):
        part = split // 2
        arrived(tag + "a2R")
        pass_on(tag + "a3", buf, left_x, other_row, 0, part, "R")
        arrived(tag + "a2L")
        pass_on(tag + "a3", buf, right_x, other_row, part, part, "L")

    def gather_end(tag):
        for name in ("a1R", "a1L", "b0Y", "b1lY", "b1rY", "a3R", "a3L", "b2rY", "b2lY"):
            arrived(tag + name)

    def in_row(x, start, count):
        return pl.ds(pl.multiple_of(x * rows + start, 16), count)

    def pass_row(name, x, start, count, where):
        send(name, lambda: (gat_g.at[in_row(x, start, count)],) * 2, where)

    def grad_start():
        pass_row("g0R0", my_x, 0, half, "R")
        pass_row("g0L1", my_x, half, half, "L")
        pass_row("g0R1", my_x, half, half, "R")
        pass_row("g0L0", my_x, 0, half, "L")

    def grad_near():
        arrived("g0R0")
        pass_row("g1R", left_x, 0, half, "R")
        arrived("g0L1")
        pass_row("g1L", right_x, half, half, "L")

    def grad_end():
        for name in ("g0R1", "g0L0", "g1R", "g1L"):
            arrived(name)

    wo_pieces = 8

    def swap_wo(pieces):
        for piece in pieces:
            here = pl.ds(piece * (width // wo_pieces), width // wo_pieces)
            send(f"wo{piece}", lambda here=here: (wo_hbm.at[here], wo_y.at[here]), "Y")

    def wo_arrived():
        for piece in range(wo_pieces):
            arrived(f"wo{piece}")

    def swap_d_attn(x, name):
        send(
            "da" + name,
            lambda: (d_send.at[in_row(x, 0, rows)], g_ref.at[at(x, my_y, 0, rows)]),
            "Y",
        )

    def swap_attn(x, name):
        send(
            "at" + name,
            lambda: (attn.at[at(x, other_row, 0, rows)], attn_y.at[in_row(x, 0, rows)]),
            "Y",
        )

    places = {}
    cursor = 0
    for name, count in (
        ("a0R0", quarter),
        ("a0L0", quarter),
        ("a0R1", quarter),
        ("a0L1", quarter),
        ("a1R0", half),
        ("a1L0", half),
        ("a1R1", half),
        ("a1L1", half),
        ("a2Y", half),
        ("b0Yf", half),
        ("b0Yr", half),
        ("b0Yl", half),
        ("b0Ym", half),
        ("b1R", quarter),
        ("b1L", quarter),
        ("b2R", half),
        ("b2L", half),
    ):
        places[name] = (cursor, count)
        cursor += count
    places.update({"f0R": (0, half), "f0L": (half, half), "f1R": (rows, rows), "f1L": (2 * rows, rows)})

    def to(name, place, offset, part, recv, here, count, where):
        start = places[place][0] + offset
        send(name, lambda: (part.at[here()], recv.at[pl.ds(start, count)]), where)

    def add_in(part, recv, place, here):
        start, count = places[place]
        part[here, :] = (
            part[here, :].astype(F32) + recv[pl.ds(start, count), :].astype(F32)
        ).astype(BF16)

    def to_b(place, x, y, start, count, where, suffix="", offset=0):
        to(
            "RB" + place + suffix,
            place,
            offset,
            part_b,
            recv_b,
            lambda: at(x, y, start, count),
            count,
            where,
        )

    def reduce_far():
        for w, y in ((1, other_row), (0, own_row)):
            to_b(f"a0R{w}", far_x, y, 0, quarter, "R")
            to_b(f"a0L{w}", far_x, y, quarter, quarter, "L")
        to_b("b0Yf", far_x, other_row, half, half, "Y")

    def reduce_right():
        to_b("b0Yr", right_x, other_row, half, half, "Y")
        for w, y in ((1, other_row), (0, own_row)):
            to_b(f"a1R{w}", right_x, y, quarter, quarter, "R", "i", quarter)

    def reduce_left():
        to_b("b0Yl", left_x, other_row, half, half, "Y")
        for w, y in ((1, other_row), (0, own_row)):
            to_b(f"a1L{w}", left_x, y, 0, quarter, "L", "i", 0)

    def reduce_mine():
        to_b("b0Ym", my_x, other_row, half, half, "Y")

    def reduce_near_a():
        for w, y in ((1, other_row), (0, own_row)):
            arrived(f"RBa0R{w}")
            add_in(part_b, recv_b, f"a0R{w}", at(right_x, y, 0, quarter))
            to_b(f"a1R{w}", right_x, y, 0, quarter, "R", "d", 0)
            arrived(f"RBa0L{w}")
            add_in(part_b, recv_b, f"a0L{w}", at(left_x, y, quarter, quarter))
            to_b(f"a1L{w}", left_x, y, quarter, quarter, "L", "d", quarter)

    def reduce_far_b():
        arrived("RBb0Yf")
        add_in(part_b, recv_b, "b0Yf", at(far_x, own_row, half, half))
        to_b("b1R", far_x, own_row, half, quarter, "R")
        to_b("b1L", far_x, own_row, half + quarter, quarter, "L")
        arrived("RBb0Yr")
        add_in(part_b, recv_b, "b0Yr", at(right_x, own_row, half, half))
        to_b("b2R", right_x, own_row, half + quarter, quarter, "R", "i", quarter)
        arrived("RBb0Yl")
        add_in(part_b, recv_b, "b0Yl", at(left_x, own_row, half, half))
        to_b("b2L", left_x, own_row, half, quarter, "L", "i", 0)

    def arrived_both(name):
        arrived(name + "i")
        arrived(name + "d")

    def reduce_cross_a():
        for place in ("a1R1", "a1L1"):
            arrived_both("RB" + place)
            add_in(part_b, recv_b, place, at(my_x, other_row, 0, half))
        to_b("a2Y", my_x, other_row, 0, half, "Y")

    def reduce_near_b():
        arrived("RBb1R")
        add_in(part_b, recv_b, "b1R", at(right_x, own_row, half, quarter))
        to_b("b2R", right_x, own_row, half, quarter, "R", "d", 0)
        arrived("RBb1L")
        add_in(part_b, recv_b, "b1L", at(left_x, own_row, half + quarter, quarter))
        to_b("b2L", left_x, own_row, half + quarter, quarter, "L", "d", quarter)

    def last_a():
        arrived_both("RBa1R0")
        arrived_both("RBa1L0")
        arrived("RBa2Y")
        return ("a1R0", "a1L0", "a2Y")

    def last_b():
        arrived_both("RBb2R")
        arrived_both("RBb2L")
        arrived("RBb0Ym")
        return ("b2R", "b2L", "b0Ym")

    def to_f(place, x, start, where, suffix="", offset=0):
        to(
            "RF" + place + suffix,
            place,
            offset,
            part_f,
            recv_f,
            lambda: in_row(x, start, half),
            half,
            where,
        )

    def row_far():
        to_f("f0R", far_x, 0, "R")
        to_f("f0L", far_x, half, "L")

    def row_right():
        to_f("f1R", right_x, half, "R", "i", half)

    def row_left():
        to_f("f1L", left_x, 0, "L", "i", 0)

    def row_near():
        arrived("RFf0R")
        add_in(part_f, recv_f, "f0R", in_row(right_x, 0, half))
        to_f("f1R", right_x, 0, "R", "d", 0)
        arrived("RFf0L")
        add_in(part_f, recv_f, "f0L", in_row(left_x, half, half))
        to_f("f1L", left_x, half, "L", "d", half)

    step_rows = 16

    def total_of(part, base, recv, spans, offset):
        total = part[pl.ds(pl.multiple_of(base + offset, step_rows), step_rows), :].astype(F32)
        for start in spans:
            total += recv[pl.ds(start + offset, step_rows), :].astype(F32)
        return total

    def finish_act(start, name):
        spans = [places[place][0] + start for place in ("f1R", "f1L")]

        def body(i, carry):
            offset = pl.multiple_of(i * step_rows, step_rows)
            here = pl.ds(start + offset, step_rows)
            total = total_of(part_f, my_x * rows + start, recv_f, spans, offset)
            out_f[here, :] = (x_fwd[here, :] + total).astype(BF16)
            return carry

        lax.fori_loop(0, half // step_rows, body, 0)
        send(name, lambda: (out_f.at[pl.ds(start, half)], act_ref.at[pl.ds(start, half)]), "N")

    def finish_grad(names, start, name):
        spans = [places[place][0] for place in names]

        def body(i, carry):
            offset = pl.multiple_of(i * step_rows, step_rows)
            here = pl.ds(start + offset, step_rows)
            saved = x_bwd[here, :]
            inv_rms = lax.rsqrt(jnp.mean(saved * saved, -1, keepdims=True) + 1e-05)
            total = total_of(part_b, slot(my_x, my_y) * rows + start, recv_b, spans, offset)
            gain_grad = total * gain_ref[...]
            mean = jnp.mean(saved * gain_grad, -1, keepdims=True)
            d_input = inv_rms * gain_grad - saved * (inv_rms * inv_rms * inv_rms * mean)
            out_b[here, :] = (grad[here, :] + d_input).astype(BF16)
            return carry

        lax.fori_loop(0, half // step_rows, body, 0)
        send(name, lambda: (out_b.at[pl.ds(start, half)], dgrad_ref.at[pl.ds(start, half)]), "P")

    block = 256
    blocks = length // block

    def rotated(values, here, sign):
        out = values * cos[here, :]
        turned = pltpu.roll(values, HD // 2, 1) * sin[here, :]
        return out + turned if sign > 0 else out - turned

    def project(buf):
        def body(i, carry):
            here = pl.ds(pl.multiple_of(i * block, block), block)
            normed = buf[here, :]
            query = dot_nn(normed, wq[...])
            key = dot_nn(normed, wk[...])
            for h in range(heads):
                head = slice(h * HD, (h + 1) * HD)
                q_ref[here, head] = rotated(query[:, head], here, 1).astype(BF16)
                turned = rotated(key[:, head], here, 1)
                k_ref[here, head] = turned.astype(BF16)
                kt_ref[head, here] = turned.T.astype(BF16)
            value = dot_nn(normed, wv[...])
            v_ref[here, :] = value.astype(BF16)
            vt_ref[:, here] = value.T.astype(BF16)
            return carry

        lax.fori_loop(0, blocks, body, 0)

    def project_grad():
        def cross(x, carry):
            here = in_row(x, 0, rows)
            d_send[here, :] = dot_nn(gat_g[here, :], wo_y[...]).astype(BF16)
            return carry

        lax.fori_loop(0, n_x, cross, 0)
        for name, x in others.items():
            swap_d_attn(x, name)

        def own(x, carry):
            there = at(x, my_y, 0, rows)
            g_ref[there, :] = dot_nn(gat_g[in_row(x, 0, rows), :], wo[...]).astype(BF16)
            return carry

        lax.fori_loop(0, n_x, own, 0)

    def run_actions(actions, h, i):
        for number, todo in actions.items():
            if number // blocks == h:

                @pl.when(i == number % blocks)
                def _(todo=todo):
                    for act in todo:
                        act()

    def exponentials(h, here):
        head = slice(h * HD, (h + 1) * HD)
        scores = dot_nt(k_ref[:, head], q_ref[here, head])
        top = jnp.max(scores, axis=0, keepdims=True)
        weights = jnp.exp2((scores - top) * (SCALE * LOG2E))
        return weights, 1.0 / jnp.sum(weights, axis=0, keepdims=True)

    def attend_back(actions):
        for h in range(heads):
            head = slice(h * HD, (h + 1) * HD)
            dk_acc[...] = jnp.zeros_like(dk_acc)
            dv_acc[...] = jnp.zeros_like(dv_acc)

            def body(i, carry, h=h, head=head):
                run_actions(actions, h, i)
                here = pl.ds(pl.multiple_of(i * block, block), block)
                weights, inverse = exponentials(h, here)
                probs = weights * inverse
                d_out = g_ref[here, head]
                dv_acc[...] += dot_nn(probs.astype(BF16), d_out)
                d_probs = dot_nt(v_ref[:, head], d_out)
                delta = jnp.sum(probs * d_probs, axis=0, keepdims=True)
                d_scores = (probs * (d_probs - delta) * SCALE).astype(BF16)
                dk_acc[...] += dot_nn(d_scores, q_ref[here, head])
                d_query = dot_nn(kt_ref[head, :], d_scores).T
                dqkv[here, head] = rotated(d_query, here, -1).astype(BF16)
                return carry

            lax.fori_loop(0, blocks, body, 0)

            def close(i, carry, h=h):
                here = pl.ds(pl.multiple_of(i * block, block), block)
                d_key = rotated(dk_acc[here, :], here, -1)
                dqkv[here, feats + h * HD : feats + (h + 1) * HD] = d_key.astype(BF16)
                dqkv[here, 2 * feats + h * HD : 2 * feats + (h + 1) * HD] = dv_acc[here, :].astype(BF16)
                return carry

            lax.fori_loop(0, blocks, close, 0)

    def attend(x):
        def body(i, carry):
            here = pl.ds(pl.multiple_of(x * block, block), block)
            for h in range(heads):
                head = slice(h * HD, (h + 1) * HD)
                weights, inverse = exponentials(h, here)
                out = dot_nn(vt_ref[head, :], weights.astype(BF16)) * inverse
                attn[here, head] = out.T.astype(BF16)
            return carry

        lax.fori_loop(0, 1, body, 0)

    columns = 512

    def multiply_out_b(x):
        here = pl.ds(pl.multiple_of(x * block, block), block)

        def body(i, carry):
            there = pl.ds(pl.multiple_of(i * columns, columns), columns)
            part_b[here, there] = dot_nn(dqkv[here, :], w3t[:, there]).astype(BF16)
            return carry

        lax.fori_loop(0, width // columns, body, 0)

    def multiply_out_f(x):
        here = in_row(x, 0, rows)
        both = jnp.concatenate([attn[at(x, my_y, 0, rows), :], attn_y[here, :]], 1)

        def body(i, carry):
            there = pl.ds(pl.multiple_of(i * columns, columns), columns)
            part_f[here, there] = dot_nn(both, wot[:, there]).astype(BF16)
            return carry

        lax.fori_loop(0, width // columns, body, 0)

    def transpose_into(source, target, offset):
        def body(i, carry):
            here = pl.ds(pl.multiple_of(i * feats, feats), feats)
            target[offset : offset + feats, here] = source[here, :].T
            return carry

        lax.fori_loop(0, width // feats, body, 0)

    split_b, split_f = half + quarter, half
    loads[0].wait()
    normalize_into(x_bwd, gat_b)
    pl.semaphore_wait(barrier, len(devices))
    gather_start("B", gat_b, split_b)
    swap_wo(range(0, 4))
    loads[1].wait()
    round_into(grad, gat_g)
    loads[2].wait()
    normalize_into(x_fwd, gat_f)
    gather_near_a("B", gat_b, split_b)
    gather_cross_a("B", gat_b, split_b)
    grad_start()
    for index in range(3, 9):
        loads[index].wait()
    transpose_into(wq, w3t, 0)
    gather_near_b("B", gat_b, split_b)
    swap_wo(range(4, 8))
    gather_far_b("B", gat_b, split_b)
    transpose_into(wk, w3t, feats)
    gather_far_a("B", gat_b, split_b)
    grad_near()
    gather_start("F", gat_f, split_f)
    transpose_into(wv, w3t, 2 * feats)
    transpose_into(wo, wot, 0)
    gather_end("B")
    project(gat_b)
    gather_near_a("F", gat_f, split_f)
    gather_cross_a("F", gat_f, split_f)
    wo_arrived()
    grad_end()
    project_grad()
    transpose_into(wo_y, wot, feats)
    gather_near_b("F", gat_f, split_f)
    for name in others:
        arrived("da" + name)
    attend_back(
        {
            2: [lambda: gather_far_b("F", gat_f, split_f)],
            3: [lambda: gather_far_a("F", gat_f, split_f)],
        }
    )

    multiply_out_b(far_x)
    reduce_far()
    multiply_out_b(right_x)
    reduce_right()
    multiply_out_b(left_x)
    reduce_left()
    multiply_out_b(my_x)
    reduce_mine()
    gather_end("F")
    project(gat_f)
    reduce_near_a()
    attend(far_x)
    swap_attn(far_x, "f")
    reduce_far_b()
    attend(right_x)
    swap_attn(right_x, "r")
    attend(left_x)
    swap_attn(left_x, "l")
    reduce_cross_a()
    arrived("atf")
    multiply_out_f(far_x)
    row_far()
    reduce_near_b()
    arrived("atr")
    multiply_out_f(right_x)
    row_right()
    arrived("atl")
    multiply_out_f(left_x)
    row_left()
    attend(my_x)
    swap_attn(my_x, "m")
    row_near()
    finish_grad(last_a(), 0, "PBa")
    finish_grad(last_b(), half, "PBb")
    arrived("atm")
    multiply_out_f(my_x)
    arrived("RFf1Rd")
    arrived("RFf1Li")
    finish_act(0, "PFa")
    arrived("RFf1Ri")
    arrived("RFf1Ld")
    finish_act(half, "PFb")
    for name in ("PBa", "PBb", "PFa", "PFb"):
        arrived(name)
    for name in copies:
        describe(name).wait_send()


def shards(x_fwd, x_bwd, grad_in, gain, w_query, w_key, w_value, w_out):
    rows, width = x_fwd.shape[1:]
    feats = w_query.shape[2]
    length = rows * lax.axis_size("seq")
    cosine, sine = (jnp.asarray(table) for table in rope_constants(length))
    anywhere = pl.BlockSpec(memory_space=pl.ANY)
    vmem = pltpu.VMEM
    n_copies = 104
    act, dgrad = pl.pallas_call(
        kernel,
        out_shape=[jax.ShapeDtypeStruct((rows, width), BF16)] * 2,
        in_specs=[anywhere] * 3 + [pl.BlockSpec(memory_space=pltpu.VMEM)] + [anywhere] * 6,
        out_specs=[anywhere] * 2,
        scratch_shapes=[vmem((rows, width), F32)] * 3
        + [vmem((width, feats), BF16)] * 5
        + [vmem((length, HD), F32)] * 2
        + [vmem((3 * feats, width), BF16), vmem((2 * feats, width), BF16)]
        + [vmem((length, width), BF16)] * 2
        + [vmem((length // 2, width), BF16)]
        + [vmem((length, feats), BF16)] * 4
        + [vmem((feats, length), BF16)] * 2
        + [vmem((length, HD), F32)] * 2
        + [vmem((length, 3 * feats), BF16), vmem((length, feats), BF16)]
        + [vmem((length // 2, feats), BF16)] * 2
        + [vmem((length, width), BF16), vmem((length // 2, width), BF16)]
        + [vmem((rows * 7, width), BF16), vmem((rows * 3, width), BF16)]
        + [vmem((rows, width), BF16)] * 2
        + [
            pltpu.SemaphoreType.DMA((9,)),
            pltpu.SemaphoreType.DMA((n_copies,)),
            pltpu.SemaphoreType.DMA((n_copies,)),
        ],
        compiler_params=pltpu.CompilerParams(
            collective_id=0, has_side_effects=True, vmem_limit_bytes=67_043_328
        ),
        name="relay_attention",
    )(
        x_fwd[0],
        x_bwd[0],
        grad_in[0],
        gain,
        w_query[0],
        w_key[0],
        w_value[0],
        w_out[0],
        cosine,
        sine,
    )
    return (act.astype(F32)[None], dgrad.astype(F32)[None])


def solution(mesh):
    placed = (
        P("pipe", "seq", None),
        P("pipe", "seq", None),
        P("pipe", "seq", None),
        P("pipe", None),
        P("pipe", None, "seq"),
        P("pipe", None, "seq"),
        P("pipe", None, "seq"),
        P("pipe", None, "seq"),
    )
    return jax.shard_map(
        shards,
        mesh=mesh,
        in_specs=placed,
        out_specs=(P("pipe", "seq", None), P("pipe", "seq", None)),
        check_vma=False,
    )
```

```python
import math

import jax
import jax.numpy as jnp
import numpy as np
from jax import lax
from jax.experimental import pallas as pl
from jax.experimental.pallas import tpu as pltpu
from jax.sharding import PartitionSpec as P

HD = 128
MESH = pl.DeviceIdType.MESH
F32 = jnp.float32
BF16 = jnp.bfloat16
SCALE = HD ** (-0.5)
LOG2E = math.log2(math.e)


def rope_constants(length):
    inverse = 10000.0 ** (-(np.arange(HD // 2, dtype=np.float64) * 2.0 / HD))
    angles = np.arange(length, dtype=np.float64)[:, None] * inverse[None, :]
    cosine, sine = np.cos(angles), np.sin(angles)
    return (
        np.concatenate([cosine, cosine], 1).astype(np.float32),
        np.concatenate([-sine, sine], 1).astype(np.float32),
    )


def dot_nn(left, right):
    return jnp.dot(left, right, preferred_element_type=F32)


def dot_nt(left, right):
    return lax.dot_general(left, right, (((1,), (1,)), ((), ())), preferred_element_type=F32)


def kernel(
    x_fwd_hbm,
    x_bwd_hbm,
    grad_hbm,
    gain_ref,
    wq_hbm,
    wk_hbm,
    wv_hbm,
    wo_hbm,
    cos_hbm,
    sin_hbm,
    act_ref,
    dgrad_ref,
    x_fwd,
    x_bwd,
    grad,
    wq,
    wk,
    wv,
    wo,
    wo_y,
    cos,
    sin,
    w3t,
    wot,
    gat_f,
    gat_b,
    gat_g,
    q_ref,
    k_ref,
    v_ref,
    g_ref,
    kt_ref,
    vt_ref,
    dk_acc,
    dv_acc,
    dqkv,
    attn,
    attn_y,
    d_send,
    part_b,
    part_f,
    recv_b,
    recv_f,
    out_b,
    out_f,
    load_sem,
    send_sem,
    recv_sem,
):
    rows = x_fwd.shape[0]
    half, quarter = rows // 2, rows // 4
    length, width = gat_f.shape
    feats = wq.shape[1]
    heads = feats // HD
    pipe, seq = lax.axis_index("pipe"), lax.axis_index("seq")
    n_pipe = lax.axis_size("pipe")
    n_x = lax.axis_size("seq") // 2
    my_x, my_y = lax.div(seq, 2), lax.rem(seq, 2)
    left_x, right_x, far_x = (lax.rem(my_x + step, n_x) for step in (n_x - 1, 1, 2))
    own_row, other_row = my_y, 1 - my_y

    def slot(x, y):
        return x * 2 + y

    def at(x, y, start, count):
        return pl.ds(pl.multiple_of(slot(x, y) * rows + start, 16), count)

    others = {"f": far_x, "r": right_x, "l": left_x, "m": my_x}
    devices = {
        "L": (pipe, slot(left_x, my_y)),
        "R": (pipe, slot(right_x, my_y)),
        "Y": (pipe, slot(my_x, 1 - my_y)),
        "N": (lax.rem(pipe + 1, n_pipe), seq),
        "P": (lax.rem(pipe + n_pipe - 1, n_pipe), seq),
    }

    loads = {}

    def load(index, src, dst):
        loads[index] = pltpu.make_async_copy(src, dst, load_sem.at[index])
        loads[index].start()

    load(0, x_bwd_hbm, x_bwd)
    load(1, grad_hbm, grad)

    barrier = pltpu.get_barrier_semaphore()
    for device in devices.values():
        pl.semaphore_signal(barrier, inc=1, device_id=device, device_id_type=MESH)

    copies = {}

    def describe(name):
        index, refs, where = copies[name]
        src, dst = refs()
        return pltpu.make_async_remote_copy(
            src_ref=src,
            dst_ref=dst,
            send_sem=send_sem.at[index],
            recv_sem=recv_sem.at[index],
            device_id=devices[where],
            device_id_type=MESH,
        )

    def send(name, refs, where):
        copies[name] = (len(copies), refs, where)
        describe(name).start()

    def arrived(name):
        describe(name).wait_recv()

    def normalize_into(source, target):
        def body(i, carry):
            here = pl.ds(pl.multiple_of(i * quarter, quarter), quarter)
            values = source[here, :]
            inv_rms = lax.rsqrt(jnp.mean(values * values, -1, keepdims=True) + 1e-05)
            there = at(my_x, my_y, i * quarter, quarter)
            target[there, :] = (values * inv_rms * gain_ref[...]).astype(BF16)
            return carry

        lax.fori_loop(0, rows // quarter, body, 0)

    def round_into(source, target):
        def body(i, carry):
            here = pl.ds(pl.multiple_of(i * quarter, quarter), quarter)
            target[in_row(my_x, i * quarter, quarter), :] = source[here, :].astype(BF16)
            return carry

        lax.fori_loop(0, rows // quarter, body, 0)

    def pass_on(tag, buf, x, y, start, count, where):
        send(tag + where, lambda: (buf.at[at(x, y, start, count)],) * 2, where)

    def gather_start_a(tag, buf, split):
        pass_on(tag + "a0", buf, my_x, my_y, 0, split, "Y")
        for where in "LR":
            pass_on(tag + "a0", buf, my_x, my_y, 0, split, where)

    def gather_start_b(tag, buf, split):
        for where in "LRY":
            pass_on(tag + "b0", buf, my_x, my_y, split, rows - split, where)

    def gather_near_a(tag, buf, split):
        part = split // 2
        arrived(tag + "a0R")
        pass_on(tag + "a1", buf, left_x, my_y, 0, part, "R")
        arrived(tag + "a0L")
        pass_on(tag + "a1", buf, right_x, my_y, part, part, "L")

    def gather_cross_a(tag, buf, split):
        arrived(tag + "a0Y")
        for where in "LR":
            pass_on(tag + "a2", buf, my_x, other_row, 0, split, where)

    def gather_near_b(tag, buf, split):
        part = (rows - split) // 2
        arrived(tag + "b0R")
        pass_on(tag + "b1", buf, left_x, my_y, split, part, "R")
        arrived(tag + "b0L")
        pass_on(tag + "b1", buf, right_x, my_y, split + part, part, "L")

    def gather_near_by(tag, buf, split):
        pass_on(tag + "b1l", buf, left_x, my_y, split, rows - split, "Y")
        pass_on(tag + "b1r", buf, right_x, my_y, split, rows - split, "Y")

    def gather_far_b(tag, buf, split):
        part = (rows - split) // 2
        arrived(tag + "b1R")
        pass_on(tag + "b2r", buf, far_x, my_y, split, part, "Y")
        arrived(tag + "b1L")
        pass_on(tag + "b2l", buf, far_x, my_y, split + part, part, "Y")

    def gather_far_a(tag, buf, split):
        part = split // 2
        arrived(tag + "a2R")
        pass_on(tag + "a3", buf, left_x, other_row, 0, part, "R")
        arrived(tag + "a2L")
        pass_on(tag + "a3", buf, right_x, other_row, part, part, "L")

    def gather_end(tag):
        for name in ("a1R", "a1L", "b0Y", "b1lY", "b1rY", "a3R", "a3L", "b2rY", "b2lY"):
            arrived(tag + name)

    def in_row(x, start, count):
        return pl.ds(pl.multiple_of(x * rows + start, 16), count)

    def pass_row(name, x, start, count, where):
        send(name, lambda: (gat_g.at[in_row(x, start, count)],) * 2, where)

    def grad_start():
        pass_row("g0R0", my_x, 0, half, "R")
        pass_row("g0L1", my_x, half, half, "L")
        pass_row("g0R1", my_x, half, half, "R")
        pass_row("g0L0", my_x, 0, half, "L")

    def grad_near():
        arrived("g0R0")
        pass_row("g1R", left_x, 0, half, "R")
        arrived("g0L1")
        pass_row("g1L", right_x, half, half, "L")

    def grad_end():
        for name in ("g0R1", "g0L0", "g1R", "g1L"):
            arrived(name)

    wo_pieces = 8

    def swap_wo(pieces):
        for piece in pieces:
            here = pl.ds(piece * (width // wo_pieces), width // wo_pieces)
            send(f"wo{piece}", lambda here=here: (wo_hbm.at[here], wo_y.at[here]), "Y")

    def wo_arrived():
        for piece in range(wo_pieces):
            arrived(f"wo{piece}")

    def swap_d_attn(x, name):
        send(
            "da" + name,
            lambda: (d_send.at[in_row(x, 0, rows)], g_ref.at[at(x, my_y, 0, rows)]),
            "Y",
        )

    def swap_attn(x, name):
        send(
            "at" + name,
            lambda: (attn.at[at(x, other_row, 0, rows)], attn_y.at[in_row(x, 0, rows)]),
            "Y",
        )

    split_r = 64
    rest = rows - split_r
    part_a, part_c = split_r // 2, rest // 2
    groups = ((0, 64), (64, 32), (96, 32))
    places = {}
    cursor = 0
    for name, count in (
        ("a0R0", part_a),
        ("a0L0", part_a),
        ("a0R1", part_a),
        ("a0L1", part_a),
        ("a1R0", split_r),
        ("a1L0", split_r),
        ("a1R1", split_r),
        ("a1L1", split_r),
        ("a2Y", split_r),
        ("b0Yf", rest),
        ("b0Yr", rest),
        ("b0Yl", rest),
        ("b0Ym", rest),
        ("b1R", part_c),
        ("b1L", part_c),
        ("b2R", rest),
        ("b2L", rest),
    ):
        places[name] = (cursor, count)
        cursor += count
    for number, (start, count) in enumerate(groups):
        places[f"f0R{number}"] = (start // 2, count // 2)
        places[f"f0L{number}"] = (half + start // 2, count // 2)
    places.update({"f1R": (rows, rows), "f1L": (2 * rows, rows)})

    def to(name, place, offset, part, recv, here, count, where):
        start = places[place][0] + offset
        send(name, lambda: (part.at[here()], recv.at[pl.ds(start, count)]), where)

    def add_in(part, recv, place, here):
        start, count = places[place]
        part[here, :] = (
            part[here, :].astype(F32) + recv[pl.ds(start, count), :].astype(F32)
        ).astype(BF16)

    def to_b(place, x, y, start, count, where, suffix="", offset=0):
        to(
            "RB" + place + suffix,
            place,
            offset,
            part_b,
            recv_b,
            lambda: at(x, y, start, count),
            count,
            where,
        )

    def reduce_far():
        for w, y in ((1, other_row), (0, own_row)):
            to_b(f"a0R{w}", far_x, y, 0, part_a, "R")
            to_b(f"a0L{w}", far_x, y, part_a, part_a, "L")

    def reduce_cross(name, x):
        to_b("b0Y" + name, x, other_row, split_r, rest, "Y")

    def reduce_right():
        for w, y in ((1, other_row), (0, own_row)):
            to_b(f"a1R{w}", right_x, y, part_a, part_a, "R", "i", part_a)

    def reduce_left():
        for w, y in ((1, other_row), (0, own_row)):
            to_b(f"a1L{w}", left_x, y, 0, part_a, "L", "i", 0)

    def reduce_near_a(w):
        y = (own_row, other_row)[w]
        arrived(f"RBa0R{w}")
        add_in(part_b, recv_b, f"a0R{w}", at(right_x, y, 0, part_a))
        to_b(f"a1R{w}", right_x, y, 0, part_a, "R", "d", 0)
        arrived(f"RBa0L{w}")
        add_in(part_b, recv_b, f"a0L{w}", at(left_x, y, part_a, part_a))
        to_b(f"a1L{w}", left_x, y, part_a, part_a, "L", "d", part_a)

    def reduce_far_b():
        arrived("RBb0Yf")
        add_in(part_b, recv_b, "b0Yf", at(far_x, own_row, split_r, rest))
        to_b("b1R", far_x, own_row, split_r, part_c, "R")
        to_b("b1L", far_x, own_row, split_r + part_c, part_c, "L")

    def reduce_side_b():
        arrived("RBb0Yr")
        add_in(part_b, recv_b, "b0Yr", at(right_x, own_row, split_r, rest))
        to_b("b2R", right_x, own_row, split_r + part_c, part_c, "R", "i", part_c)
        arrived("RBb0Yl")
        add_in(part_b, recv_b, "b0Yl", at(left_x, own_row, split_r, rest))
        to_b("b2L", left_x, own_row, split_r, part_c, "L", "i", 0)

    def arrived_both(name):
        arrived(name + "i")
        arrived(name + "d")

    def reduce_cross_a():
        for place in ("a1R1", "a1L1"):
            arrived_both("RB" + place)
            add_in(part_b, recv_b, place, at(my_x, other_row, 0, split_r))
        to_b("a2Y", my_x, other_row, 0, split_r, "Y")

    def reduce_near_b():
        arrived("RBb1R")
        add_in(part_b, recv_b, "b1R", at(right_x, own_row, split_r, part_c))
        to_b("b2R", right_x, own_row, split_r, part_c, "R", "d", 0)
        arrived("RBb1L")
        add_in(part_b, recv_b, "b1L", at(left_x, own_row, split_r + part_c, part_c))
        to_b("b2L", left_x, own_row, split_r + part_c, part_c, "L", "d", part_c)

    def to_f(place, x, start, count, where, name, offset=0):
        to(
            "RF" + name,
            place,
            offset,
            part_f,
            recv_f,
            lambda: in_row(x, start, count),
            count,
            where,
        )

    def row_far():
        for number, (start, count) in enumerate(groups):
            to_f(f"f0R{number}", far_x, start, count // 2, "R", f"f0R{number}")
            to_f(f"f0L{number}", far_x, start + count // 2, count // 2, "L", f"f0L{number}")

    def row_right(number):
        start, part = groups[number][0], groups[number][1] // 2
        to_f("f1R", right_x, start + part, part, "R", f"f1R{number}i", start + part)

    def row_left(number):
        start, part = groups[number][0], groups[number][1] // 2
        to_f("f1L", left_x, start, part, "L", f"f1L{number}i", start)

    def row_near(number):
        start, part = groups[number][0], groups[number][1] // 2
        arrived(f"RFf0R{number}")
        add_in(part_f, recv_f, f"f0R{number}", in_row(right_x, start, part))
        to_f("f1R", right_x, start, part, "R", f"f1R{number}d", start)
        arrived(f"RFf0L{number}")
        add_in(part_f, recv_f, f"f0L{number}", in_row(left_x, start + part, part))
        to_f("f1L", left_x, start + part, part, "L", f"f1L{number}d", start + part)

    step_rows = 16

    def total_of(part, base, recv, spans, offset):
        total = part[pl.ds(pl.multiple_of(base + offset, step_rows), step_rows), :].astype(F32)
        for start in spans:
            total += recv[pl.ds(start + offset, step_rows), :].astype(F32)
        return total

    def finish_act(number):
        start, count = groups[number]
        spans = [places[place][0] + start for place in ("f1R", "f1L")]
        arrived_both(f"RFf1R{number}")
        arrived_both(f"RFf1L{number}")

        def body(i, carry):
            offset = pl.multiple_of(i * step_rows, step_rows)
            here = pl.ds(start + offset, step_rows)
            total = total_of(part_f, my_x * rows + start, recv_f, spans, offset)
            out_f[here, :] = (x_fwd[here, :] + total).astype(BF16)
            return carry

        lax.fori_loop(0, count // step_rows, body, 0)
        send(
            f"PF{number}",
            lambda: (out_f.at[pl.ds(start, count)], act_ref.at[pl.ds(start, count)]),
            "N",
        )

    def finish_grad(last):
        if last:
            start, count, names = split_r, rest, ("b2R", "b2L", "b0Ym")
            arrived_both("RBb2R")
            arrived_both("RBb2L")
            arrived("RBb0Ym")
        else:
            start, count, names = 0, split_r, ("a1R0", "a1L0", "a2Y")
            arrived_both("RBa1R0")
            arrived_both("RBa1L0")
            arrived("RBa2Y")
        spans = [places[place][0] for place in names]

        def body(i, carry):
            offset = pl.multiple_of(i * step_rows, step_rows)
            here = pl.ds(start + offset, step_rows)
            saved = x_bwd[here, :]
            inv_rms = lax.rsqrt(jnp.mean(saved * saved, -1, keepdims=True) + 1e-05)
            total = total_of(part_b, slot(my_x, my_y) * rows + start, recv_b, spans, offset)
            gain_grad = total * gain_ref[...]
            mean = jnp.mean(saved * gain_grad, -1, keepdims=True)
            d_input = inv_rms * gain_grad - saved * (inv_rms * inv_rms * inv_rms * mean)
            out_b[here, :] = (grad[here, :] + d_input).astype(BF16)
            return carry

        lax.fori_loop(0, count // step_rows, body, 0)
        send(
            f"PB{last}",
            lambda: (out_b.at[pl.ds(start, count)], dgrad_ref.at[pl.ds(start, count)]),
            "P",
        )

    block = 256
    blocks = length // block

    def rotated(values, here, sign):
        out = values * cos[here, :]
        turned = pltpu.roll(values, HD // 2, 1) * sin[here, :]
        return out + turned if sign > 0 else out - turned

    def project(buf):
        def body(i, carry):
            here = pl.ds(pl.multiple_of(i * block, block), block)
            normed = buf[here, :]
            query = dot_nn(normed, wq[...])
            key = dot_nn(normed, wk[...])
            for h in range(heads):
                head = slice(h * HD, (h + 1) * HD)
                q_ref[here, head] = rotated(query[:, head], here, 1).astype(BF16)
                turned = rotated(key[:, head], here, 1)
                k_ref[here, head] = turned.astype(BF16)
                kt_ref[head, here] = turned.T.astype(BF16)
            value = dot_nn(normed, wv[...])
            v_ref[here, :] = value.astype(BF16)
            vt_ref[:, here] = value.T.astype(BF16)
            return carry

        lax.fori_loop(0, blocks, body, 0)

    def project_grad_cross():
        def body(x, carry):
            here = in_row(x, 0, rows)
            d_send[here, :] = dot_nn(gat_g[here, :], wo_y[...]).astype(BF16)
            return carry

        lax.fori_loop(0, n_x, body, 0)
        for name, x in others.items():
            swap_d_attn(x, name)

    def project_grad_own():
        def body(x, carry):
            there = at(x, my_y, 0, rows)
            g_ref[there, :] = dot_nn(gat_g[in_row(x, 0, rows), :], wo[...]).astype(BF16)
            return carry

        lax.fori_loop(0, n_x, body, 0)

    def d_attn_arrived():
        for name in others:
            arrived("da" + name)

    def run_actions(actions, h, i):
        for number, todo in actions.items():
            if number // blocks == h:

                @pl.when(i == number % blocks)
                def _(todo=todo):
                    for act in todo:
                        act()

    def exponentials(h, here):
        head = slice(h * HD, (h + 1) * HD)
        scores = dot_nt(k_ref[:, head], q_ref[here, head])
        top = jnp.max(scores, axis=0, keepdims=True)
        weights = jnp.exp2((scores - top) * (SCALE * LOG2E))
        return weights, 1.0 / jnp.sum(weights, axis=0, keepdims=True)

    def attend_back(actions):
        for h in range(heads):
            head = slice(h * HD, (h + 1) * HD)
            dk_acc[...] = jnp.zeros_like(dk_acc)
            dv_acc[...] = jnp.zeros_like(dv_acc)

            def body(i, carry, h=h, head=head):
                run_actions(actions, h, i)
                here = pl.ds(pl.multiple_of(i * block, block), block)
                weights, inverse = exponentials(h, here)
                probs = weights * inverse
                d_out = g_ref[here, head]
                dv_acc[...] += dot_nn(probs.astype(BF16), d_out)
                d_probs = dot_nt(v_ref[:, head], d_out)
                delta = jnp.sum(probs * d_probs, axis=0, keepdims=True)
                d_scores = (probs * (d_probs - delta) * SCALE).astype(BF16)
                dk_acc[...] += dot_nn(d_scores, q_ref[here, head])
                d_query = dot_nn(kt_ref[head, :], d_scores).T
                dqkv[here, head] = rotated(d_query, here, -1).astype(BF16)
                return carry

            lax.fori_loop(0, blocks, body, 0)

            def close(i, carry, h=h):
                here = pl.ds(pl.multiple_of(i * block, block), block)
                d_key = rotated(dk_acc[here, :], here, -1)
                dqkv[here, feats + h * HD : feats + (h + 1) * HD] = d_key.astype(BF16)
                dqkv[here, 2 * feats + h * HD : 2 * feats + (h + 1) * HD] = dv_acc[here, :].astype(BF16)
                return carry

            lax.fori_loop(0, blocks, close, 0)

    def attend(x):
        def body(i, carry):
            here = pl.ds(pl.multiple_of(x * block, block), block)
            for h in range(heads):
                head = slice(h * HD, (h + 1) * HD)
                weights, inverse = exponentials(h, here)
                out = dot_nn(vt_ref[head, :], weights.astype(BF16)) * inverse
                attn[here, head] = out.T.astype(BF16)
            return carry

        lax.fori_loop(0, 1, body, 0)

    columns = 512

    def multiply_out_b(x):
        here = pl.ds(pl.multiple_of(x * block, block), block)

        def body(i, carry):
            there = pl.ds(pl.multiple_of(i * columns, columns), columns)
            part_b[here, there] = dot_nn(dqkv[here, :], w3t[:, there]).astype(BF16)
            return carry

        lax.fori_loop(0, width // columns, body, 0)

    def multiply_out_f(x):
        here = in_row(x, 0, rows)
        both = jnp.concatenate([attn[at(x, my_y, 0, rows), :], attn_y[here, :]], 1)

        def body(i, carry):
            there = pl.ds(pl.multiple_of(i * columns, columns), columns)
            part_f[here, there] = dot_nn(both, wot[:, there]).astype(BF16)
            return carry

        lax.fori_loop(0, width // columns, body, 0)

    def transpose_into(source, target, offset):
        def body(i, carry):
            here = pl.ds(pl.multiple_of(i * feats, feats), feats)
            target[offset : offset + feats, here] = source[here, :].T
            return carry

        lax.fori_loop(0, width // feats, body, 0)

    split_b, split_f = 96, 64
    pl.semaphore_wait(barrier, len(devices))
    swap_wo(range(0, 1))
    loads[0].wait()
    load(2, x_fwd_hbm, x_fwd)
    load(3, wo_hbm, wo)
    load(4, wq_hbm, wq)
    load(5, wk_hbm, wk)
    load(6, wv_hbm, wv)
    load(7, cos_hbm, cos)
    load(8, sin_hbm, sin)
    normalize_into(x_bwd, gat_b)
    gather_start_b("B", gat_b, split_b)
    loads[1].wait()
    round_into(grad, gat_g)
    gather_start_a("B", gat_b, split_b)
    loads[2].wait()
    normalize_into(x_fwd, gat_f)
    for index in range(3, 9):
        loads[index].wait()
    gather_near_b("B", gat_b, split_b)
    swap_wo(range(6, 7))
    gather_near_by("B", gat_b, split_b)
    grad_start()
    swap_wo(range(5, 6))
    transpose_into(wk, w3t, feats)
    swap_wo(range(7, 8))
    swap_wo(range(1, 2))
    swap_wo(range(3, 4))
    gather_cross_a("B", gat_b, split_b)
    gather_far_b("B", gat_b, split_b)
    grad_near()
    swap_wo(range(4, 5))
    swap_wo(range(2, 3))
    gather_far_a("B", gat_b, split_b)
    gather_near_a("B", gat_b, split_b)
    gather_start_b("F", gat_f, split_f)
    grad_end()
    project_grad_own()
    wo_arrived()
    project_grad_cross()
    gather_start_a("F", gat_f, split_f)
    transpose_into(wo_y, wot, feats)
    transpose_into(wo, wot, 0)
    gather_end("B")
    project(gat_b)
    transpose_into(wq, w3t, 0)
    gather_near_b("F", gat_f, split_f)
    d_attn_arrived()
    attend_back(
        {
            1: [
                lambda: transpose_into(wv, w3t, 2 * feats),
                lambda: gather_near_by("F", gat_f, split_f),
            ],
            3: [
                lambda: gather_cross_a("F", gat_f, split_f),
            ],
            4: [
                lambda: gather_near_a("F", gat_f, split_f),
            ],
            7: [
                lambda: gather_far_b("F", gat_f, split_f),
                lambda: gather_far_a("F", gat_f, split_f),
            ],
        }
    )
    multiply_out_b(far_x)
    reduce_far()
    multiply_out_b(left_x)
    multiply_out_b(right_x)
    reduce_left()
    reduce_cross("f", far_x)
    reduce_right()
    reduce_cross("r", right_x)
    gather_end("F")
    project(gat_f)
    reduce_near_a(1)
    attend(far_x)
    swap_attn(far_x, "f")
    reduce_cross("l", left_x)
    attend(left_x)
    swap_attn(left_x, "l")
    reduce_far_b()
    attend(right_x)
    reduce_near_a(0)
    multiply_out_b(my_x)
    swap_attn(right_x, "r")
    reduce_cross("m", my_x)
    arrived("atf")
    multiply_out_f(far_x)
    row_far()
    reduce_side_b()
    arrived("atl")
    multiply_out_f(left_x)
    reduce_near_b()
    arrived("atr")
    multiply_out_f(right_x)
    row_near(0)
    row_right(0)
    attend(my_x)
    row_left(0)
    row_right(2)
    swap_attn(my_x, "m")
    reduce_cross_a()
    arrived("atm")
    multiply_out_f(my_x)
    row_near(2)
    row_left(2)
    finish_grad(True)
    row_near(1)
    finish_act(0)
    row_right(1)
    row_left(1)
    finish_grad(False)
    finish_act(2)
    finish_act(1)
    for name in ("PBFalse", "PBTrue", "PF0", "PF1", "PF2"):
        arrived(name)
    for name in copies:
        describe(name).wait_send()


def shards(x_fwd, x_bwd, grad_in, gain, w_query, w_key, w_value, w_out):
    rows, width = x_fwd.shape[1:]
    feats = w_query.shape[2]
    length = rows * lax.axis_size("seq")
    cosine, sine = (jnp.asarray(table) for table in rope_constants(length))
    anywhere = pl.BlockSpec(memory_space=pl.ANY)
    vmem = pltpu.VMEM
    n_copies = 112
    act, dgrad = pl.pallas_call(
        kernel,
        out_shape=[jax.ShapeDtypeStruct((rows, width), BF16)] * 2,
        in_specs=[anywhere] * 3 + [pl.BlockSpec(memory_space=pltpu.VMEM)] + [anywhere] * 6,
        out_specs=[anywhere] * 2,
        scratch_shapes=[vmem((rows, width), F32)] * 3
        + [vmem((width, feats), BF16)] * 5
        + [vmem((length, HD), F32)] * 2
        + [vmem((3 * feats, width), BF16), vmem((2 * feats, width), BF16)]
        + [vmem((length, width), BF16)] * 2
        + [vmem((length // 2, width), BF16)]
        + [vmem((length, feats), BF16)] * 4
        + [vmem((feats, length), BF16)] * 2
        + [vmem((length, HD), F32)] * 2
        + [vmem((length, 3 * feats), BF16), vmem((length, feats), BF16)]
        + [vmem((length // 2, feats), BF16)] * 2
        + [vmem((length, width), BF16), vmem((length // 2, width), BF16)]
        + [vmem((rows * 7, width), BF16), vmem((rows * 3, width), BF16)]
        + [vmem((rows, width), BF16)] * 2
        + [
            pltpu.SemaphoreType.DMA((9,)),
            pltpu.SemaphoreType.DMA((n_copies,)),
            pltpu.SemaphoreType.DMA((n_copies,)),
        ],
        compiler_params=pltpu.CompilerParams(
            collective_id=0, has_side_effects=True, vmem_limit_bytes=67_043_328
        ),
        name="relay_attention",
    )(
        x_fwd[0],
        x_bwd[0],
        grad_in[0],
        gain,
        w_query[0],
        w_key[0],
        w_value[0],
        w_out[0],
        cosine,
        sine,
    )
    return (act.astype(F32)[None], dgrad.astype(F32)[None])


def solution(mesh):
    placed = (
        P("pipe", "seq", None),
        P("pipe", "seq", None),
        P("pipe", "seq", None),
        P("pipe", None),
        P("pipe", None, "seq"),
        P("pipe", None, "seq"),
        P("pipe", None, "seq"),
        P("pipe", None, "seq"),
    )
    return jax.shard_map(
        shards,
        mesh=mesh,
        in_specs=placed,
        out_specs=(P("pipe", "seq", None), P("pipe", "seq", None)),
        check_vma=False,
    )
```

```python
import math

import jax
import jax.numpy as jnp
import numpy as np
from jax import lax
from jax.experimental import pallas as pl
from jax.experimental.pallas import tpu as pltpu
from jax.sharding import PartitionSpec as P

HD = 128
MESH = pl.DeviceIdType.MESH
F32 = jnp.float32
BF16 = jnp.bfloat16
SCALE = HD ** (-0.5)
LOG2E = math.log2(math.e)


def rope_constants(length):
    inverse = 10000.0 ** (-(np.arange(HD // 2, dtype=np.float64) * 2.0 / HD))
    angles = np.arange(length, dtype=np.float64)[:, None] * inverse[None, :]
    cosine, sine = np.cos(angles), np.sin(angles)
    return (
        np.concatenate([cosine, cosine], 1).astype(np.float32),
        np.concatenate([-sine, sine], 1).astype(np.float32),
    )


def dot_nn(left, right):
    return jnp.dot(left, right, preferred_element_type=F32)


def dot_nt(left, right):
    return lax.dot_general(left, right, (((1,), (1,)), ((), ())), preferred_element_type=F32)


def kernel(
    x_fwd_hbm,
    x_bwd_hbm,
    grad_hbm,
    gain_ref,
    wq_hbm,
    wk_hbm,
    wv_hbm,
    wo_hbm,
    cos_hbm,
    sin_hbm,
    act_ref,
    dgrad_ref,
    x_fwd,
    x_bwd,
    grad,
    wq,
    wk,
    wv,
    wo,
    wo_y,
    cos,
    sin,
    w3t,
    wot,
    gat_f,
    gat_b,
    gat_g,
    q_ref,
    k_ref,
    v_ref,
    g_ref,
    kt_ref,
    vt_ref,
    dk_acc,
    dv_acc,
    dqkv,
    attn,
    attn_y,
    d_send,
    part_b,
    part_f,
    recv_b,
    recv_f,
    out_b,
    out_f,
    load_sem,
    send_sem,
    recv_sem,
):
    rows = x_fwd.shape[0]
    half, quarter = rows // 2, rows // 4
    length, width = gat_f.shape
    feats = wq.shape[1]
    heads = feats // HD
    pipe, seq = lax.axis_index("pipe"), lax.axis_index("seq")
    n_pipe = lax.axis_size("pipe")
    n_x = lax.axis_size("seq") // 2
    my_x, my_y = lax.div(seq, 2), lax.rem(seq, 2)
    left_x, right_x, far_x = (lax.rem(my_x + step, n_x) for step in (n_x - 1, 1, 2))
    own_row, other_row = my_y, 1 - my_y

    def slot(x, y):
        return x * 2 + y

    def at(x, y, start, count):
        return pl.ds(pl.multiple_of(slot(x, y) * rows + start, 16), count)

    others = {"f": far_x, "r": right_x, "l": left_x, "m": my_x}
    devices = {
        "L": (pipe, slot(left_x, my_y)),
        "R": (pipe, slot(right_x, my_y)),
        "Y": (pipe, slot(my_x, 1 - my_y)),
        "N": (lax.rem(pipe + 1, n_pipe), seq),
        "P": (lax.rem(pipe + n_pipe - 1, n_pipe), seq),
    }

    loads = {}

    def load(index, src, dst):
        loads[index] = pltpu.make_async_copy(src, dst, load_sem.at[index])
        loads[index].start()

    load(0, x_bwd_hbm, x_bwd)
    load(1, grad_hbm, grad)

    barrier = pltpu.get_barrier_semaphore()
    for device in devices.values():
        pl.semaphore_signal(barrier, inc=1, device_id=device, device_id_type=MESH)

    copies = {}

    def describe(name):
        index, refs, where = copies[name]
        src, dst = refs()
        return pltpu.make_async_remote_copy(
            src_ref=src,
            dst_ref=dst,
            send_sem=send_sem.at[index],
            recv_sem=recv_sem.at[index],
            device_id=devices[where],
            device_id_type=MESH,
        )

    def send(name, refs, where):
        copies[name] = (len(copies), refs, where)
        describe(name).start()

    def arrived(name):
        describe(name).wait_recv()

    def normalize_into(source, target):
        def body(i, carry):
            here = pl.ds(pl.multiple_of(i * quarter, quarter), quarter)
            values = source[here, :]
            inv_rms = lax.rsqrt(jnp.mean(values * values, -1, keepdims=True) + 1e-05)
            there = at(my_x, my_y, i * quarter, quarter)
            target[there, :] = (values * inv_rms * gain_ref[...]).astype(BF16)
            return carry

        lax.fori_loop(0, rows // quarter, body, 0)

    def round_into(source, target):
        def body(i, carry):
            here = pl.ds(pl.multiple_of(i * quarter, quarter), quarter)
            target[in_row(my_x, i * quarter, quarter), :] = source[here, :].astype(BF16)
            return carry

        lax.fori_loop(0, rows // quarter, body, 0)

    def pass_on(tag, buf, x, y, start, count, where):
        send(tag + where, lambda: (buf.at[at(x, y, start, count)],) * 2, where)

    def gather_start_a(tag, buf, split):
        pass_on(tag + "a0", buf, my_x, my_y, 0, split, "Y")
        for where in "LR":
            pass_on(tag + "a0", buf, my_x, my_y, 0, split, where)

    def gather_start_b(tag, buf, split):
        for where in "LRY":
            pass_on(tag + "b0", buf, my_x, my_y, split, rows - split, where)

    def gather_near_a(tag, buf, split):
        part = split // 2
        arrived(tag + "a0R")
        pass_on(tag + "a1", buf, left_x, my_y, 0, part, "R")
        arrived(tag + "a0L")
        pass_on(tag + "a1", buf, right_x, my_y, part, part, "L")

    def gather_cross_a(tag, buf, split):
        arrived(tag + "a0Y")
        for where in "LR":
            pass_on(tag + "a2", buf, my_x, other_row, 0, split, where)

    def gather_near_b(tag, buf, split):
        part = (rows - split) // 2
        arrived(tag + "b0R")
        pass_on(tag + "b1", buf, left_x, my_y, split, part, "R")
        arrived(tag + "b0L")
        pass_on(tag + "b1", buf, right_x, my_y, split + part, part, "L")

    def gather_near_by(tag, buf, split):
        pass_on(tag + "b1l", buf, left_x, my_y, split, rows - split, "Y")
        pass_on(tag + "b1r", buf, right_x, my_y, split, rows - split, "Y")

    def gather_far_b(tag, buf, split):
        part = (rows - split) // 2
        arrived(tag + "b1R")
        pass_on(tag + "b2r", buf, far_x, my_y, split, part, "Y")
        arrived(tag + "b1L")
        pass_on(tag + "b2l", buf, far_x, my_y, split + part, part, "Y")

    def gather_far_a(tag, buf, split):
        part = split // 2
        arrived(tag + "a2R")
        pass_on(tag + "a3", buf, left_x, other_row, 0, part, "R")
        arrived(tag + "a2L")
        pass_on(tag + "a3", buf, right_x, other_row, part, part, "L")

    def gather_end(tag):
        for name in ("a1R", "a1L", "b0Y", "b1lY", "b1rY", "a3R", "a3L", "b2rY", "b2lY"):
            arrived(tag + name)

    def in_row(x, start, count):
        return pl.ds(pl.multiple_of(x * rows + start, 16), count)

    def pass_row(name, x, start, count, where):
        send(name, lambda: (gat_g.at[in_row(x, start, count)],) * 2, where)

    def grad_start():
        pass_row("g0R0", my_x, 0, half, "R")
        pass_row("g0L1", my_x, half, half, "L")
        pass_row("g0R1", my_x, half, half, "R")
        pass_row("g0L0", my_x, 0, half, "L")

    def grad_near():
        arrived("g0R0")
        pass_row("g1R", left_x, 0, half, "R")
        arrived("g0L1")
        pass_row("g1L", right_x, half, half, "L")

    def grad_end():
        for name in ("g0R1", "g0L0", "g1R", "g1L"):
            arrived(name)

    wo_pieces = 8

    def swap_wo(pieces):
        for piece in pieces:
            here = pl.ds(piece * (width // wo_pieces), width // wo_pieces)
            send(f"wo{piece}", lambda here=here: (wo_hbm.at[here], wo_y.at[here]), "Y")

    def wo_arrived():
        for piece in range(wo_pieces):
            arrived(f"wo{piece}")

    def swap_d_attn(x, name):
        send(
            "da" + name,
            lambda: (d_send.at[in_row(x, 0, rows)], g_ref.at[at(x, my_y, 0, rows)]),
            "Y",
        )

    def swap_attn(x, name):
        send(
            "at" + name,
            lambda: (attn.at[at(x, other_row, 0, rows)], attn_y.at[in_row(x, 0, rows)]),
            "Y",
        )

    split_r = 64
    rest = rows - split_r
    part_a, part_c = split_r // 2, rest // 2
    groups = ((0, 64), (64, 32), (96, 32))
    places = {}
    cursor = 0
    for name, count in (
        ("a0R0", part_a),
        ("a0L0", part_a),
        ("a0R1", part_a),
        ("a0L1", part_a),
        ("a1R0", split_r),
        ("a1L0", split_r),
        ("a1R1", split_r),
        ("a1L1", split_r),
        ("a2Y", split_r),
        ("b0Yf", rest),
        ("b0Yr", rest),
        ("b0Yl", rest),
        ("b0Ym", rest),
        ("b1R", part_c),
        ("b1L", part_c),
        ("b2R", rest),
        ("b2L", rest),
    ):
        places[name] = (cursor, count)
        cursor += count
    for number, (start, count) in enumerate(groups):
        places[f"f0R{number}"] = (start // 2, count // 2)
        places[f"f0L{number}"] = (half + start // 2, count // 2)
    places.update({"f1R": (rows, rows), "f1L": (2 * rows, rows)})

    def to(name, place, offset, part, recv, here, count, where):
        start = places[place][0] + offset
        send(name, lambda: (part.at[here()], recv.at[pl.ds(start, count)]), where)

    def add_in(part, recv, place, here):
        start, count = places[place]
        part[here, :] = (
            part[here, :].astype(F32) + recv[pl.ds(start, count), :].astype(F32)
        ).astype(BF16)

    def to_b(place, x, y, start, count, where, suffix="", offset=0):
        to(
            "RB" + place + suffix,
            place,
            offset,
            part_b,
            recv_b,
            lambda: at(x, y, start, count),
            count,
            where,
        )

    def reduce_far():
        for w, y in ((1, other_row), (0, own_row)):
            to_b(f"a0R{w}", far_x, y, 0, part_a, "R")
            to_b(f"a0L{w}", far_x, y, part_a, part_a, "L")

    def reduce_cross(name, x):
        to_b("b0Y" + name, x, other_row, split_r, rest, "Y")

    def reduce_right():
        for w, y in ((1, other_row), (0, own_row)):
            to_b(f"a1R{w}", right_x, y, part_a, part_a, "R", "i", part_a)

    def reduce_left():
        for w, y in ((1, other_row), (0, own_row)):
            to_b(f"a1L{w}", left_x, y, 0, part_a, "L", "i", 0)

    def reduce_near_a(w):
        y = (own_row, other_row)[w]
        arrived(f"RBa0R{w}")
        add_in(part_b, recv_b, f"a0R{w}", at(right_x, y, 0, part_a))
        to_b(f"a1R{w}", right_x, y, 0, part_a, "R", "d", 0)
        arrived(f"RBa0L{w}")
        add_in(part_b, recv_b, f"a0L{w}", at(left_x, y, part_a, part_a))
        to_b(f"a1L{w}", left_x, y, part_a, part_a, "L", "d", part_a)

    def reduce_far_b():
        arrived("RBb0Yf")
        add_in(part_b, recv_b, "b0Yf", at(far_x, own_row, split_r, rest))
        to_b("b1R", far_x, own_row, split_r, part_c, "R")
        to_b("b1L", far_x, own_row, split_r + part_c, part_c, "L")

    def reduce_side_b():
        arrived("RBb0Yr")
        add_in(part_b, recv_b, "b0Yr", at(right_x, own_row, split_r, rest))
        to_b("b2R", right_x, own_row, split_r + part_c, part_c, "R", "i", part_c)
        arrived("RBb0Yl")
        add_in(part_b, recv_b, "b0Yl", at(left_x, own_row, split_r, rest))
        to_b("b2L", left_x, own_row, split_r, part_c, "L", "i", 0)

    def arrived_both(name):
        arrived(name + "i")
        arrived(name + "d")

    def reduce_cross_a():
        for place in ("a1R1", "a1L1"):
            arrived_both("RB" + place)
            add_in(part_b, recv_b, place, at(my_x, other_row, 0, split_r))
        to_b("a2Y", my_x, other_row, 0, split_r, "Y")

    def reduce_near_b():
        arrived("RBb1R")
        add_in(part_b, recv_b, "b1R", at(right_x, own_row, split_r, part_c))
        to_b("b2R", right_x, own_row, split_r, part_c, "R", "d", 0)
        arrived("RBb1L")
        add_in(part_b, recv_b, "b1L", at(left_x, own_row, split_r + part_c, part_c))
        to_b("b2L", left_x, own_row, split_r + part_c, part_c, "L", "d", part_c)

    def to_f(place, x, start, count, where, name, offset=0):
        to(
            "RF" + name,
            place,
            offset,
            part_f,
            recv_f,
            lambda: in_row(x, start, count),
            count,
            where,
        )

    def row_far():
        for number, (start, count) in enumerate(groups):
            to_f(f"f0R{number}", far_x, start, count // 2, "R", f"f0R{number}")
            to_f(f"f0L{number}", far_x, start + count // 2, count // 2, "L", f"f0L{number}")

    def row_right(number):
        start, part = groups[number][0], groups[number][1] // 2
        to_f("f1R", right_x, start + part, part, "R", f"f1R{number}i", start + part)

    def row_left(number):
        start, part = groups[number][0], groups[number][1] // 2
        to_f("f1L", left_x, start, part, "L", f"f1L{number}i", start)

    def row_near(number):
        start, part = groups[number][0], groups[number][1] // 2
        arrived(f"RFf0R{number}")
        add_in(part_f, recv_f, f"f0R{number}", in_row(right_x, start, part))
        to_f("f1R", right_x, start, part, "R", f"f1R{number}d", start)
        arrived(f"RFf0L{number}")
        add_in(part_f, recv_f, f"f0L{number}", in_row(left_x, start + part, part))
        to_f("f1L", left_x, start + part, part, "L", f"f1L{number}d", start + part)

    step_rows = 16

    def total_of(part, base, recv, spans, offset):
        total = part[pl.ds(pl.multiple_of(base + offset, step_rows), step_rows), :].astype(F32)
        for start in spans:
            total += recv[pl.ds(start + offset, step_rows), :].astype(F32)
        return total

    def finish_act(number):
        start, count = groups[number]
        spans = [places[place][0] + start for place in ("f1R", "f1L")]
        arrived_both(f"RFf1R{number}")
        arrived_both(f"RFf1L{number}")

        def body(i, carry):
            offset = pl.multiple_of(i * step_rows, step_rows)
            here = pl.ds(start + offset, step_rows)
            total = total_of(part_f, my_x * rows + start, recv_f, spans, offset)
            out_f[here, :] = (x_fwd[here, :] + total).astype(BF16)
            return carry

        piece = count // 2
        for part in range(2):
            lax.fori_loop(part * piece // step_rows, (part + 1) * piece // step_rows, body, 0)
            here = pl.ds(start + part * piece, piece)
            send(f"PF{number}{part}", lambda here=here: (out_f.at[here], act_ref.at[here]), "N")

    def finish_grad(last):
        if last:
            start, count, names = split_r, rest, ("b2R", "b2L", "b0Ym")
            arrived_both("RBb2R")
            arrived_both("RBb2L")
            arrived("RBb0Ym")
        else:
            start, count, names = 0, split_r, ("a1R0", "a1L0", "a2Y")
            arrived_both("RBa1R0")
            arrived_both("RBa1L0")
            arrived("RBa2Y")
        spans = [places[place][0] for place in names]

        def body(i, carry):
            offset = pl.multiple_of(i * step_rows, step_rows)
            here = pl.ds(start + offset, step_rows)
            saved = x_bwd[here, :]
            inv_rms = lax.rsqrt(jnp.mean(saved * saved, -1, keepdims=True) + 1e-05)
            total = total_of(part_b, slot(my_x, my_y) * rows + start, recv_b, spans, offset)
            gain_grad = total * gain_ref[...]
            mean = jnp.mean(saved * gain_grad, -1, keepdims=True)
            d_input = inv_rms * gain_grad - saved * (inv_rms * inv_rms * inv_rms * mean)
            out_b[here, :] = (grad[here, :] + d_input).astype(BF16)
            return carry

        lax.fori_loop(0, count // step_rows, body, 0)
        send(
            f"PB{last}",
            lambda: (out_b.at[pl.ds(start, count)], dgrad_ref.at[pl.ds(start, count)]),
            "P",
        )

    block = 256
    blocks = length // block

    def rotated(values, here, sign):
        out = values * cos[here, :]
        turned = pltpu.roll(values, HD // 2, 1) * sin[here, :]
        return out + turned if sign > 0 else out - turned

    def project(buf):
        def body(i, carry):
            here = pl.ds(pl.multiple_of(i * block, block), block)
            normed = buf[here, :]
            query = dot_nn(normed, wq[...])
            key = dot_nn(normed, wk[...])
            for h in range(heads):
                head = slice(h * HD, (h + 1) * HD)
                q_ref[here, head] = rotated(query[:, head], here, 1).astype(BF16)
                turned = rotated(key[:, head], here, 1)
                k_ref[here, head] = turned.astype(BF16)
                kt_ref[head, here] = turned.T.astype(BF16)
            value = dot_nn(normed, wv[...])
            v_ref[here, :] = value.astype(BF16)
            vt_ref[:, here] = value.T.astype(BF16)
            return carry

        lax.fori_loop(0, blocks, body, 0)

    def project_grad_cross():
        def body(x, carry):
            here = in_row(x, 0, rows)
            d_send[here, :] = dot_nn(gat_g[here, :], wo_y[...]).astype(BF16)
            return carry

        lax.fori_loop(0, n_x, body, 0)
        for name, x in others.items():
            swap_d_attn(x, name)

    def project_grad_own():
        def body(x, carry):
            there = at(x, my_y, 0, rows)
            g_ref[there, :] = dot_nn(gat_g[in_row(x, 0, rows), :], wo[...]).astype(BF16)
            return carry

        lax.fori_loop(0, n_x, body, 0)

    def d_attn_arrived():
        for name in others:
            arrived("da" + name)

    def run_actions(actions, h, i):
        for number, todo in actions.items():
            if number // blocks == h:

                @pl.when(i == number % blocks)
                def _(todo=todo):
                    for act in todo:
                        act()

    def exponentials(h, here):
        head = slice(h * HD, (h + 1) * HD)
        scores = dot_nt(k_ref[:, head], q_ref[here, head])
        top = jnp.max(scores, axis=0, keepdims=True)
        weights = jnp.exp2((scores - top) * (SCALE * LOG2E))
        return weights, 1.0 / jnp.sum(weights, axis=0, keepdims=True)

    def attend_back(actions):
        for h in range(heads):
            head = slice(h * HD, (h + 1) * HD)
            dk_acc[...] = jnp.zeros_like(dk_acc)
            dv_acc[...] = jnp.zeros_like(dv_acc)

            def body(i, carry, h=h, head=head):
                run_actions(actions, h, i)
                here = pl.ds(pl.multiple_of(i * block, block), block)
                weights, inverse = exponentials(h, here)
                probs = weights * inverse
                d_out = g_ref[here, head]
                dv_acc[...] += dot_nn(probs.astype(BF16), d_out)
                d_probs = dot_nt(v_ref[:, head], d_out)
                delta = jnp.sum(probs * d_probs, axis=0, keepdims=True)
                d_scores = (probs * (d_probs - delta) * SCALE).astype(BF16)
                dk_acc[...] += dot_nn(d_scores, q_ref[here, head])
                d_query = dot_nn(kt_ref[head, :], d_scores).T
                dqkv[here, head] = rotated(d_query, here, -1).astype(BF16)
                return carry

            lax.fori_loop(0, blocks, body, 0)

            def close(i, carry, h=h):
                here = pl.ds(pl.multiple_of(i * block, block), block)
                d_key = rotated(dk_acc[here, :], here, -1)
                dqkv[here, feats + h * HD : feats + (h + 1) * HD] = d_key.astype(BF16)
                dqkv[here, 2 * feats + h * HD : 2 * feats + (h + 1) * HD] = dv_acc[here, :].astype(BF16)
                return carry

            lax.fori_loop(0, blocks, close, 0)

    def attend(x):
        def body(i, carry):
            here = pl.ds(pl.multiple_of(x * block, block), block)
            for h in range(heads):
                head = slice(h * HD, (h + 1) * HD)
                weights, inverse = exponentials(h, here)
                out = dot_nn(vt_ref[head, :], weights.astype(BF16)) * inverse
                attn[here, head] = out.T.astype(BF16)
            return carry

        lax.fori_loop(0, 1, body, 0)

    columns = 512

    def multiply_out_b(x):
        here = pl.ds(pl.multiple_of(x * block, block), block)

        def body(i, carry):
            there = pl.ds(pl.multiple_of(i * columns, columns), columns)
            part_b[here, there] = dot_nn(dqkv[here, :], w3t[:, there]).astype(BF16)
            return carry

        lax.fori_loop(0, width // columns, body, 0)

    def multiply_out_f(x):
        here = in_row(x, 0, rows)
        both = jnp.concatenate([attn[at(x, my_y, 0, rows), :], attn_y[here, :]], 1)

        def body(i, carry):
            there = pl.ds(pl.multiple_of(i * columns, columns), columns)
            part_f[here, there] = dot_nn(both, wot[:, there]).astype(BF16)
            return carry

        lax.fori_loop(0, width // columns, body, 0)

    def transpose_into(source, target, offset):
        def body(i, carry):
            here = pl.ds(pl.multiple_of(i * feats, feats), feats)
            target[offset : offset + feats, here] = source[here, :].T
            return carry

        lax.fori_loop(0, width // feats, body, 0)

    split_b, split_f = 96, 64
    pl.semaphore_wait(barrier, len(devices))
    swap_wo(range(0, 1))
    loads[0].wait()
    load(2, x_fwd_hbm, x_fwd)
    load(3, wo_hbm, wo)
    load(4, wq_hbm, wq)
    load(5, wk_hbm, wk)
    load(6, wv_hbm, wv)
    load(7, cos_hbm, cos)
    load(8, sin_hbm, sin)
    normalize_into(x_bwd, gat_b)
    gather_start_b("B", gat_b, split_b)
    loads[1].wait()
    round_into(grad, gat_g)
    gather_start_a("B", gat_b, split_b)
    loads[2].wait()
    normalize_into(x_fwd, gat_f)
    for index in range(3, 9):
        loads[index].wait()
    gather_near_b("B", gat_b, split_b)
    swap_wo(range(6, 7))
    gather_near_by("B", gat_b, split_b)
    grad_start()
    swap_wo(range(5, 6))
    transpose_into(wk, w3t, feats)
    swap_wo(range(7, 8))
    swap_wo(range(1, 2))
    swap_wo(range(3, 4))
    gather_cross_a("B", gat_b, split_b)
    gather_far_b("B", gat_b, split_b)
    grad_near()
    swap_wo(range(4, 5))
    swap_wo(range(2, 3))
    gather_far_a("B", gat_b, split_b)
    gather_near_a("B", gat_b, split_b)
    gather_start_b("F", gat_f, split_f)
    grad_end()
    project_grad_own()
    wo_arrived()
    project_grad_cross()
    gather_start_a("F", gat_f, split_f)
    transpose_into(wo_y, wot, feats)
    transpose_into(wo, wot, 0)
    gather_end("B")
    project(gat_b)
    transpose_into(wq, w3t, 0)
    gather_near_b("F", gat_f, split_f)
    d_attn_arrived()
    attend_back(
        {
            1: [
                lambda: transpose_into(wv, w3t, 2 * feats),
                lambda: gather_near_by("F", gat_f, split_f),
            ],
            3: [
                lambda: gather_cross_a("F", gat_f, split_f),
            ],
            4: [
                lambda: gather_near_a("F", gat_f, split_f),
            ],
            7: [
                lambda: gather_far_b("F", gat_f, split_f),
                lambda: gather_far_a("F", gat_f, split_f),
            ],
        }
    )
    multiply_out_b(far_x)
    reduce_far()
    multiply_out_b(left_x)
    multiply_out_b(right_x)
    reduce_left()
    reduce_cross("f", far_x)
    reduce_right()
    reduce_cross("r", right_x)
    gather_end("F")
    project(gat_f)
    reduce_near_a(1)
    attend(far_x)
    swap_attn(far_x, "f")
    reduce_cross("l", left_x)
    attend(left_x)
    swap_attn(left_x, "l")
    reduce_far_b()
    attend(right_x)
    reduce_near_a(0)
    multiply_out_b(my_x)
    swap_attn(right_x, "r")
    reduce_cross("m", my_x)
    arrived("atf")
    multiply_out_f(far_x)
    row_far()
    reduce_side_b()
    arrived("atl")
    multiply_out_f(left_x)
    reduce_near_b()
    arrived("atr")
    multiply_out_f(right_x)
    row_near(0)
    row_right(0)
    attend(my_x)
    row_left(0)
    row_right(2)
    swap_attn(my_x, "m")
    reduce_cross_a()
    arrived("atm")
    multiply_out_f(my_x)
    row_near(2)
    row_left(2)
    finish_grad(True)
    row_near(1)
    finish_act(0)
    row_right(1)
    row_left(1)
    finish_grad(False)
    finish_act(2)
    finish_act(1)
    for name in ("PBFalse", "PBTrue", "PF00", "PF01", "PF10", "PF11", "PF20", "PF21"):
        arrived(name)
    for name in copies:
        describe(name).wait_send()


def shards(x_fwd, x_bwd, grad_in, gain, w_query, w_key, w_value, w_out):
    rows, width = x_fwd.shape[1:]
    feats = w_query.shape[2]
    length = rows * lax.axis_size("seq")
    cosine, sine = (jnp.asarray(table) for table in rope_constants(length))
    hbm = pl.BlockSpec(memory_space=pltpu.HBM)
    vmem = pltpu.VMEM
    n_copies = 112
    act, dgrad = pl.pallas_call(
        kernel,
        out_shape=[jax.ShapeDtypeStruct((rows, width), BF16)] * 2,
        in_specs=[hbm] * 3 + [pl.BlockSpec(memory_space=pltpu.VMEM)] + [hbm] * 6,
        out_specs=[pl.BlockSpec(memory_space=pltpu.VMEM)] * 2,
        scratch_shapes=[vmem((rows, width), F32)] * 3
        + [vmem((width, feats), BF16)] * 5
        + [vmem((length, HD), F32)] * 2
        + [vmem((3 * feats, width), BF16), vmem((2 * feats, width), BF16)]
        + [vmem((length, width), BF16)] * 2
        + [vmem((length // 2, width), BF16)]
        + [vmem((length, feats), BF16)] * 4
        + [vmem((feats, length), BF16)] * 2
        + [vmem((length, HD), F32)] * 2
        + [vmem((length, 3 * feats), BF16), vmem((length, feats), BF16)]
        + [vmem((length // 2, feats), BF16)] * 2
        + [vmem((length, width), BF16), vmem((length // 2, width), BF16)]
        + [vmem((rows * 7, width), BF16), vmem((rows * 3, width), BF16)]
        + [vmem((rows, width), BF16)] * 2
        + [
            pltpu.SemaphoreType.DMA((9,)),
            pltpu.SemaphoreType.DMA((n_copies,)),
            pltpu.SemaphoreType.DMA((n_copies,)),
        ],
        compiler_params=pltpu.CompilerParams(
            collective_id=0, has_side_effects=True, vmem_limit_bytes=55_312_384
        ),
        name="relay_attention",
    )(
        x_fwd[0],
        x_bwd[0],
        grad_in[0],
        gain,
        w_query[0],
        w_key[0],
        w_value[0],
        w_out[0],
        cosine,
        sine,
    )
    return (act.astype(F32)[None], dgrad.astype(F32)[None])


def solution(mesh):
    placed = (
        P("pipe", "seq", None),
        P("pipe", "seq", None),
        P("pipe", "seq", None),
        P("pipe", None),
        P("pipe", None, "seq"),
        P("pipe", None, "seq"),
        P("pipe", None, "seq"),
        P("pipe", None, "seq"),
    )
    return jax.shard_map(
        shards,
        mesh=mesh,
        in_specs=placed,
        out_specs=(P("pipe", "seq", None), P("pipe", "seq", None)),
        check_vma=False,
    )
```

```python
import math

import jax
import jax.numpy as jnp
import numpy as np
from jax import lax
from jax.experimental import pallas as pl
from jax.experimental.pallas import tpu as pltpu
from jax.sharding import PartitionSpec as P

HD = 128
MESH = pl.DeviceIdType.MESH
F32 = jnp.float32
BF16 = jnp.bfloat16
SCALE = HD ** (-0.5)
LOG2E = math.log2(math.e)


def rope_constants(length):
    inverse = 10000.0 ** (-(np.arange(HD // 2, dtype=np.float64) * 2.0 / HD))
    angles = np.arange(length, dtype=np.float64)[:, None] * inverse[None, :]
    cosine, sine = np.cos(angles), np.sin(angles)
    return (
        np.concatenate([cosine, cosine], 1).astype(np.float32),
        np.concatenate([-sine, sine], 1).astype(np.float32),
    )


def dot_nn(left, right):
    return jnp.dot(left, right, preferred_element_type=F32)


def dot_nt(left, right):
    return lax.dot_general(left, right, (((1,), (1,)), ((), ())), preferred_element_type=F32)


def kernel(
    x_fwd_hbm,
    x_bwd_hbm,
    grad_hbm,
    gain_ref,
    wq_hbm,
    wk_hbm,
    wv_hbm,
    wo_hbm,
    cos_hbm,
    sin_hbm,
    act_ref,
    dgrad_ref,
    x_fwd,
    x_bwd,
    grad,
    wq,
    wk,
    wv,
    wo,
    wo_y,
    cos,
    sin,
    w3t,
    wot,
    gat_f,
    gat_b,
    gat_g,
    q_ref,
    k_ref,
    v_ref,
    g_ref,
    kt_ref,
    vt_ref,
    dk_acc,
    dv_acc,
    dqkv,
    attn,
    attn_y,
    d_send,
    part_b,
    part_f,
    recv_b,
    recv_f,
    out_b,
    out_f,
    load_sem,
    send_sem,
    recv_sem,
):
    rows = x_fwd.shape[0]
    half, quarter = rows // 2, rows // 4
    length, width = gat_f.shape
    feats = wq.shape[1]
    heads = feats // HD
    pipe, seq = lax.axis_index("pipe"), lax.axis_index("seq")
    n_pipe = lax.axis_size("pipe")
    n_x = lax.axis_size("seq") // 2
    my_x, my_y = lax.div(seq, 2), lax.rem(seq, 2)
    left_x, right_x, far_x = (lax.rem(my_x + step, n_x) for step in (n_x - 1, 1, 2))
    own_row, other_row = my_y, 1 - my_y

    def slot(x, y):
        return x * 2 + y

    def at(x, y, start, count):
        return pl.ds(pl.multiple_of(slot(x, y) * rows + start, 16), count)

    others = {"f": far_x, "r": right_x, "l": left_x, "m": my_x}
    devices = {
        "L": (pipe, slot(left_x, my_y)),
        "R": (pipe, slot(right_x, my_y)),
        "Y": (pipe, slot(my_x, 1 - my_y)),
        "N": (lax.rem(pipe + 1, n_pipe), seq),
        "P": (lax.rem(pipe + n_pipe - 1, n_pipe), seq),
    }

    loads = {}

    def load(index, src, dst):
        loads[index] = pltpu.make_async_copy(src, dst, load_sem.at[index])
        loads[index].start()

    barrier = pltpu.get_barrier_semaphore()
    for device in (devices[where] for where in "NPYLR"):
        pl.semaphore_signal(barrier, inc=1, device_id=device, device_id_type=MESH)

    load(0, x_bwd_hbm, x_bwd)
    load(1, grad_hbm, grad)

    copies = {}

    def describe(name):
        index, refs, where = copies[name]
        src, dst = refs()
        return pltpu.make_async_remote_copy(
            src_ref=src,
            dst_ref=dst,
            send_sem=send_sem.at[index],
            recv_sem=recv_sem.at[index],
            device_id=devices[where],
            device_id_type=MESH,
        )

    def send(name, refs, where):
        copies[name] = (len(copies), refs, where)
        describe(name).start()

    def arrived(name):
        describe(name).wait_recv()

    def normalize_into(source, target):
        def body(i, carry):
            here = pl.ds(pl.multiple_of(i * quarter, quarter), quarter)
            values = source[here, :]
            inv_rms = lax.rsqrt(jnp.mean(values * values, -1, keepdims=True) + 1e-05)
            there = at(my_x, my_y, i * quarter, quarter)
            target[there, :] = (values * inv_rms * gain_ref[...]).astype(BF16)
            return carry

        lax.fori_loop(0, rows // quarter, body, 0)

    def round_into(source, target):
        def body(i, carry):
            here = pl.ds(pl.multiple_of(i * quarter, quarter), quarter)
            target[in_row(my_x, i * quarter, quarter), :] = source[here, :].astype(BF16)
            return carry

        lax.fori_loop(0, rows // quarter, body, 0)

    def pass_on(tag, buf, x, y, start, count, where):
        send(tag + where, lambda: (buf.at[at(x, y, start, count)],) * 2, where)

    def gather_start_a(tag, buf, split):
        pass_on(tag + "a0", buf, my_x, my_y, 0, split, "Y")
        for where in "LR":
            pass_on(tag + "a0", buf, my_x, my_y, 0, split, where)

    def gather_start_b(tag, buf, split):
        for where in "LRY":
            pass_on(tag + "b0", buf, my_x, my_y, split, rows - split, where)

    def gather_near_a(tag, buf, split):
        part = split // 2
        arrived(tag + "a0R")
        pass_on(tag + "a1", buf, left_x, my_y, 0, part, "R")
        arrived(tag + "a0L")
        pass_on(tag + "a1", buf, right_x, my_y, part, part, "L")

    def gather_cross_a(tag, buf, split):
        arrived(tag + "a0Y")
        for where in "LR":
            pass_on(tag + "a2", buf, my_x, other_row, 0, split, where)

    def gather_near_b(tag, buf, split):
        part = (rows - split) // 2
        arrived(tag + "b0R")
        pass_on(tag + "b1", buf, left_x, my_y, split, part, "R")
        arrived(tag + "b0L")
        pass_on(tag + "b1", buf, right_x, my_y, split + part, part, "L")

    def gather_near_by(tag, buf, split):
        pass_on(tag + "b1l", buf, left_x, my_y, split, rows - split, "Y")
        pass_on(tag + "b1r", buf, right_x, my_y, split, rows - split, "Y")

    def gather_far_b(tag, buf, split):
        part = (rows - split) // 2
        arrived(tag + "b1R")
        pass_on(tag + "b2r", buf, far_x, my_y, split, part, "Y")
        arrived(tag + "b1L")
        pass_on(tag + "b2l", buf, far_x, my_y, split + part, part, "Y")

    def gather_far_a(tag, buf, split):
        part = split // 2
        arrived(tag + "a2R")
        pass_on(tag + "a3", buf, left_x, other_row, 0, part, "R")
        arrived(tag + "a2L")
        pass_on(tag + "a3", buf, right_x, other_row, part, part, "L")

    def gather_end(tag):
        for name in ("a1R", "a1L", "b0Y", "b1lY", "b1rY", "a3R", "a3L", "b2rY", "b2lY"):
            arrived(tag + name)

    def in_row(x, start, count):
        return pl.ds(pl.multiple_of(x * rows + start, 16), count)

    def pass_row(name, x, start, count, where):
        send(name, lambda: (gat_g.at[in_row(x, start, count)],) * 2, where)

    def grad_start():
        pass_row("g0R0", my_x, 0, half, "R")
        pass_row("g0L1", my_x, half, half, "L")
        pass_row("g0R1", my_x, half, half, "R")
        pass_row("g0L0", my_x, 0, half, "L")

    def grad_near():
        arrived("g0R0")
        pass_row("g1R", left_x, 0, half, "R")
        arrived("g0L1")
        pass_row("g1L", right_x, half, half, "L")

    def grad_end():
        for name in ("g0R1", "g0L0", "g1R", "g1L"):
            arrived(name)

    wo_pieces = 8

    def swap_wo(pieces):
        for piece in pieces:
            here = pl.ds(piece * (width // wo_pieces), width // wo_pieces)
            send(f"wo{piece}", lambda here=here: (wo_hbm.at[here], wo_y.at[here]), "Y")

    def wo_arrived():
        for piece in range(wo_pieces):
            arrived(f"wo{piece}")

    def swap_d_attn(x, name):
        send(
            "da" + name,
            lambda: (d_send.at[in_row(x, 0, rows)], g_ref.at[at(x, my_y, 0, rows)]),
            "Y",
        )

    def swap_attn(x, name):
        send(
            "at" + name,
            lambda: (attn.at[at(x, other_row, 0, rows)], attn_y.at[in_row(x, 0, rows)]),
            "Y",
        )

    split_r = 64
    rest = rows - split_r
    part_a, part_c = split_r // 2, rest // 2
    groups = ((0, 64), (64, 32), (96, 32))
    places = {}
    cursor = 0
    for name, count in (
        ("a0R0", part_a),
        ("a0L0", part_a),
        ("a0R1", part_a),
        ("a0L1", part_a),
        ("a1R0", split_r),
        ("a1L0", split_r),
        ("a1R1", split_r),
        ("a1L1", split_r),
        ("a2Y", split_r),
        ("b0Yf", rest),
        ("b0Yr", rest),
        ("b0Yl", rest),
        ("b0Ym", rest),
        ("b1R", part_c),
        ("b1L", part_c),
        ("b2R", rest),
        ("b2L", rest),
    ):
        places[name] = (cursor, count)
        cursor += count
    for number, (start, count) in enumerate(groups):
        places[f"f0R{number}"] = (start // 2, count // 2)
        places[f"f0L{number}"] = (half + start // 2, count // 2)
    places.update({"f1R": (rows, rows), "f1L": (2 * rows, rows)})

    def to(name, place, offset, part, recv, here, count, where):
        start = places[place][0] + offset
        send(name, lambda: (part.at[here()], recv.at[pl.ds(start, count)]), where)

    def add_in(part, recv, place, here):
        start, count = places[place]
        part[here, :] = (
            part[here, :].astype(F32) + recv[pl.ds(start, count), :].astype(F32)
        ).astype(BF16)

    def to_b(place, x, y, start, count, where, suffix="", offset=0):
        to(
            "RB" + place + suffix,
            place,
            offset,
            part_b,
            recv_b,
            lambda: at(x, y, start, count),
            count,
            where,
        )

    def reduce_far():
        for w, y in ((1, other_row), (0, own_row)):
            to_b(f"a0R{w}", far_x, y, 0, part_a, "R")
            to_b(f"a0L{w}", far_x, y, part_a, part_a, "L")

    def reduce_cross(name, x):
        to_b("b0Y" + name, x, other_row, split_r, rest, "Y")

    def reduce_right():
        for w, y in ((1, other_row), (0, own_row)):
            to_b(f"a1R{w}", right_x, y, part_a, part_a, "R", "i", part_a)

    def reduce_left():
        for w, y in ((1, other_row), (0, own_row)):
            to_b(f"a1L{w}", left_x, y, 0, part_a, "L", "i", 0)

    def reduce_near_a(w):
        y = (own_row, other_row)[w]
        arrived(f"RBa0R{w}")
        add_in(part_b, recv_b, f"a0R{w}", at(right_x, y, 0, part_a))
        to_b(f"a1R{w}", right_x, y, 0, part_a, "R", "d", 0)
        arrived(f"RBa0L{w}")
        add_in(part_b, recv_b, f"a0L{w}", at(left_x, y, part_a, part_a))
        to_b(f"a1L{w}", left_x, y, part_a, part_a, "L", "d", part_a)

    def reduce_far_b():
        arrived("RBb0Yf")
        add_in(part_b, recv_b, "b0Yf", at(far_x, own_row, split_r, rest))
        to_b("b1R", far_x, own_row, split_r, part_c, "R")
        to_b("b1L", far_x, own_row, split_r + part_c, part_c, "L")

    def reduce_side_b():
        arrived("RBb0Yr")
        add_in(part_b, recv_b, "b0Yr", at(right_x, own_row, split_r, rest))
        to_b("b2R", right_x, own_row, split_r + part_c, part_c, "R", "i", part_c)
        arrived("RBb0Yl")
        add_in(part_b, recv_b, "b0Yl", at(left_x, own_row, split_r, rest))
        to_b("b2L", left_x, own_row, split_r, part_c, "L", "i", 0)

    def arrived_both(name):
        arrived(name + "i")
        arrived(name + "d")

    def reduce_cross_a():
        for place in ("a1R1", "a1L1"):
            arrived_both("RB" + place)
            add_in(part_b, recv_b, place, at(my_x, other_row, 0, split_r))
        to_b("a2Y", my_x, other_row, 0, split_r, "Y")

    def reduce_near_b():
        arrived("RBb1R")
        add_in(part_b, recv_b, "b1R", at(right_x, own_row, split_r, part_c))
        to_b("b2R", right_x, own_row, split_r, part_c, "R", "d", 0)
        arrived("RBb1L")
        add_in(part_b, recv_b, "b1L", at(left_x, own_row, split_r + part_c, part_c))
        to_b("b2L", left_x, own_row, split_r + part_c, part_c, "L", "d", part_c)

    def to_f(place, x, start, count, where, name, offset=0):
        to(
            "RF" + name,
            place,
            offset,
            part_f,
            recv_f,
            lambda: in_row(x, start, count),
            count,
            where,
        )

    def row_far():
        for number, (start, count) in enumerate(groups):
            to_f(f"f0R{number}", far_x, start, count // 2, "R", f"f0R{number}")
            to_f(f"f0L{number}", far_x, start + count // 2, count // 2, "L", f"f0L{number}")

    def row_right(number):
        start, part = groups[number][0], groups[number][1] // 2
        to_f("f1R", right_x, start + part, part, "R", f"f1R{number}i", start + part)

    def row_left(number):
        start, part = groups[number][0], groups[number][1] // 2
        to_f("f1L", left_x, start, part, "L", f"f1L{number}i", start)

    def row_near(number):
        start, part = groups[number][0], groups[number][1] // 2
        arrived(f"RFf0R{number}")
        add_in(part_f, recv_f, f"f0R{number}", in_row(right_x, start, part))
        to_f("f1R", right_x, start, part, "R", f"f1R{number}d", start)
        arrived(f"RFf0L{number}")
        add_in(part_f, recv_f, f"f0L{number}", in_row(left_x, start + part, part))
        to_f("f1L", left_x, start + part, part, "L", f"f1L{number}d", start + part)

    step_rows = 16

    def total_of(part, base, recv, spans, offset):
        total = part[pl.ds(pl.multiple_of(base + offset, step_rows), step_rows), :].astype(F32)
        for start in spans:
            total += recv[pl.ds(start + offset, step_rows), :].astype(F32)
        return total

    def finish_act(number):
        start, count = groups[number]
        spans = [places[place][0] + start for place in ("f1R", "f1L")]
        arrived_both(f"RFf1R{number}")
        arrived_both(f"RFf1L{number}")

        def body(i, carry):
            offset = pl.multiple_of(i * step_rows, step_rows)
            here = pl.ds(start + offset, step_rows)
            total = total_of(part_f, my_x * rows + start, recv_f, spans, offset)
            out_f[here, :] = (x_fwd[here, :] + total).astype(BF16)
            return carry

        piece = count // 2
        for part in range(2):
            lax.fori_loop(part * piece // step_rows, (part + 1) * piece // step_rows, body, 0)
            here = pl.ds(start + part * piece, piece)
            send(f"PF{number}{part}", lambda here=here: (out_f.at[here], act_ref.at[here]), "N")

    def finish_grad(last):
        if last:
            start, count, names = split_r, rest, ("b2R", "b2L", "b0Ym")
            arrived_both("RBb2R")
            arrived_both("RBb2L")
            arrived("RBb0Ym")
        else:
            start, count, names = 0, split_r, ("a1R0", "a1L0", "a2Y")
            arrived_both("RBa1R0")
            arrived_both("RBa1L0")
            arrived("RBa2Y")
        spans = [places[place][0] for place in names]

        def body(i, carry):
            offset = pl.multiple_of(i * step_rows, step_rows)
            here = pl.ds(start + offset, step_rows)
            saved = x_bwd[here, :]
            inv_rms = lax.rsqrt(jnp.mean(saved * saved, -1, keepdims=True) + 1e-05)
            total = total_of(part_b, slot(my_x, my_y) * rows + start, recv_b, spans, offset)
            gain_grad = total * gain_ref[...]
            mean = jnp.mean(saved * gain_grad, -1, keepdims=True)
            d_input = inv_rms * gain_grad - saved * (inv_rms * inv_rms * inv_rms * mean)
            out_b[here, :] = (grad[here, :] + d_input).astype(BF16)
            return carry

        lax.fori_loop(0, count // step_rows, body, 0)
        send(
            f"PB{last}",
            lambda: (out_b.at[pl.ds(start, count)], dgrad_ref.at[pl.ds(start, count)]),
            "P",
        )

    block = 256
    blocks = length // block

    def rotated(values, here, sign):
        out = values * cos[here, :]
        turned = pltpu.roll(values, HD // 2, 1) * sin[here, :]
        return out + turned if sign > 0 else out - turned

    def project(buf):
        def body(i, carry):
            here = pl.ds(pl.multiple_of(i * block, block), block)
            normed = buf[here, :]
            query = dot_nn(normed, wq[...])
            key = dot_nn(normed, wk[...])
            for h in range(heads):
                head = slice(h * HD, (h + 1) * HD)
                q_ref[here, head] = rotated(query[:, head], here, 1).astype(BF16)
                turned = rotated(key[:, head], here, 1)
                k_ref[here, head] = turned.astype(BF16)
                kt_ref[head, here] = turned.T.astype(BF16)
            value = dot_nn(normed, wv[...])
            v_ref[here, :] = value.astype(BF16)
            vt_ref[:, here] = value.T.astype(BF16)
            return carry

        lax.fori_loop(0, blocks, body, 0)

    def project_grad_cross():
        def body(x, carry):
            here = in_row(x, 0, rows)
            d_send[here, :] = dot_nn(gat_g[here, :], wo_y[...]).astype(BF16)
            return carry

        lax.fori_loop(0, n_x, body, 0)
        for name, x in others.items():
            swap_d_attn(x, name)

    def project_grad_own():
        def body(x, carry):
            there = at(x, my_y, 0, rows)
            g_ref[there, :] = dot_nn(gat_g[in_row(x, 0, rows), :], wo[...]).astype(BF16)
            return carry

        lax.fori_loop(0, n_x, body, 0)

    def d_attn_arrived():
        for name in others:
            arrived("da" + name)

    def run_actions(actions, h, i):
        for number, todo in actions.items():
            if number // blocks == h:

                @pl.when(i == number % blocks)
                def _(todo=todo):
                    for act in todo:
                        act()

    def exponentials(h, here):
        head = slice(h * HD, (h + 1) * HD)
        scores = dot_nt(k_ref[:, head], q_ref[here, head])
        top = jnp.max(scores, axis=0, keepdims=True)
        weights = jnp.exp2((scores - top) * (SCALE * LOG2E))
        return weights, 1.0 / jnp.sum(weights, axis=0, keepdims=True)

    def attend_back(actions):
        for h in range(heads):
            head = slice(h * HD, (h + 1) * HD)
            dk_acc[...] = jnp.zeros_like(dk_acc)
            dv_acc[...] = jnp.zeros_like(dv_acc)

            def body(i, carry, h=h, head=head):
                run_actions(actions, h, i)
                here = pl.ds(pl.multiple_of(i * block, block), block)
                weights, inverse = exponentials(h, here)
                probs = weights * inverse
                d_out = g_ref[here, head]
                dv_acc[...] += dot_nn(probs.astype(BF16), d_out)
                d_probs = dot_nt(v_ref[:, head], d_out)
                delta = jnp.sum(probs * d_probs, axis=0, keepdims=True)
                d_scores = (probs * (d_probs - delta) * SCALE).astype(BF16)
                dk_acc[...] += dot_nn(d_scores, q_ref[here, head])
                d_query = dot_nn(kt_ref[head, :], d_scores).T
                dqkv[here, head] = rotated(d_query, here, -1).astype(BF16)
                return carry

            lax.fori_loop(0, blocks, body, 0)

            def close(i, carry, h=h):
                here = pl.ds(pl.multiple_of(i * block, block), block)
                d_key = rotated(dk_acc[here, :], here, -1)
                dqkv[here, feats + h * HD : feats + (h + 1) * HD] = d_key.astype(BF16)
                dqkv[here, 2 * feats + h * HD : 2 * feats + (h + 1) * HD] = dv_acc[here, :].astype(BF16)
                return carry

            lax.fori_loop(0, blocks, close, 0)

    def attend(x):
        def body(i, carry):
            here = pl.ds(pl.multiple_of(x * block, block), block)
            for h in range(heads):
                head = slice(h * HD, (h + 1) * HD)
                weights, inverse = exponentials(h, here)
                out = dot_nn(vt_ref[head, :], weights.astype(BF16)) * inverse
                attn[here, head] = out.T.astype(BF16)
            return carry

        lax.fori_loop(0, 1, body, 0)

    columns = 512

    def multiply_out_b(x):
        here = pl.ds(pl.multiple_of(x * block, block), block)

        def body(i, carry):
            there = pl.ds(pl.multiple_of(i * columns, columns), columns)
            part_b[here, there] = dot_nn(dqkv[here, :], w3t[:, there]).astype(BF16)
            return carry

        lax.fori_loop(0, width // columns, body, 0)

    def multiply_out_f(x):
        here = in_row(x, 0, rows)
        both = jnp.concatenate([attn[at(x, my_y, 0, rows), :], attn_y[here, :]], 1)

        def body(i, carry):
            there = pl.ds(pl.multiple_of(i * columns, columns), columns)
            part_f[here, there] = dot_nn(both, wot[:, there]).astype(BF16)
            return carry

        lax.fori_loop(0, width // columns, body, 0)

    def transpose_into(source, target, offset):
        def body(i, carry):
            here = pl.ds(pl.multiple_of(i * feats, feats), feats)
            target[offset : offset + feats, here] = source[here, :].T
            return carry

        lax.fori_loop(0, width // feats, body, 0)

    split_b, split_f = 96, 64
    pl.semaphore_wait(barrier, len(devices))
    swap_wo(range(0, 1))
    loads[0].wait()
    load(2, x_fwd_hbm, x_fwd)
    load(3, wo_hbm, wo)
    load(4, wq_hbm, wq)
    load(5, wk_hbm, wk)
    load(6, wv_hbm, wv)
    load(7, cos_hbm, cos)
    load(8, sin_hbm, sin)
    normalize_into(x_bwd, gat_b)
    gather_start_b("B", gat_b, split_b)
    loads[1].wait()
    round_into(grad, gat_g)
    gather_start_a("B", gat_b, split_b)
    loads[2].wait()
    normalize_into(x_fwd, gat_f)
    for index in range(3, 9):
        loads[index].wait()
    gather_near_b("B", gat_b, split_b)
    swap_wo(range(6, 7))
    gather_near_by("B", gat_b, split_b)
    grad_start()
    swap_wo(range(5, 6))
    transpose_into(wk, w3t, feats)
    swap_wo(range(7, 8))
    swap_wo(range(1, 2))
    swap_wo(range(3, 4))
    gather_cross_a("B", gat_b, split_b)
    gather_far_b("B", gat_b, split_b)
    grad_near()
    swap_wo(range(4, 5))
    swap_wo(range(2, 3))
    gather_far_a("B", gat_b, split_b)
    gather_near_a("B", gat_b, split_b)
    gather_start_b("F", gat_f, split_f)
    grad_end()
    project_grad_own()
    wo_arrived()
    project_grad_cross()
    gather_start_a("F", gat_f, split_f)
    transpose_into(wo_y, wot, feats)
    transpose_into(wo, wot, 0)
    gather_end("B")
    project(gat_b)
    transpose_into(wq, w3t, 0)
    gather_near_b("F", gat_f, split_f)
    d_attn_arrived()
    attend_back(
        {
            1: [
                lambda: transpose_into(wv, w3t, 2 * feats),
                lambda: gather_near_by("F", gat_f, split_f),
            ],
            3: [
                lambda: gather_cross_a("F", gat_f, split_f),
            ],
            4: [
                lambda: gather_near_a("F", gat_f, split_f),
            ],
            7: [
                lambda: gather_far_b("F", gat_f, split_f),
                lambda: gather_far_a("F", gat_f, split_f),
            ],
        }
    )
    multiply_out_b(far_x)
    reduce_far()
    multiply_out_b(left_x)
    multiply_out_b(right_x)
    reduce_left()
    reduce_cross("f", far_x)
    reduce_right()
    reduce_cross("r", right_x)
    gather_end("F")
    project(gat_f)
    reduce_near_a(1)
    attend(far_x)
    swap_attn(far_x, "f")
    reduce_cross("l", left_x)
    attend(left_x)
    swap_attn(left_x, "l")
    reduce_far_b()
    attend(right_x)
    reduce_near_a(0)
    multiply_out_b(my_x)
    swap_attn(right_x, "r")
    reduce_cross("m", my_x)
    arrived("atf")
    multiply_out_f(far_x)
    row_far()
    reduce_side_b()
    arrived("atl")
    multiply_out_f(left_x)
    reduce_near_b()
    arrived("atr")
    multiply_out_f(right_x)
    row_near(0)
    row_right(0)
    attend(my_x)
    row_left(0)
    row_right(2)
    swap_attn(my_x, "m")
    reduce_cross_a()
    arrived("atm")
    multiply_out_f(my_x)
    row_near(2)
    row_left(2)
    finish_grad(True)
    row_near(1)
    finish_act(0)
    row_right(1)
    row_left(1)
    finish_grad(False)
    finish_act(2)
    finish_act(1)
    for name in copies:
        describe(name).wait_send()
    for name in ("PBFalse", "PBTrue", "PF00", "PF01", "PF10", "PF11", "PF20", "PF21"):
        arrived(name)


def shards(x_fwd, x_bwd, grad_in, gain, w_query, w_key, w_value, w_out):
    rows, width = x_fwd.shape[1:]
    feats = w_query.shape[2]
    length = rows * lax.axis_size("seq")
    cosine, sine = (jnp.asarray(table) for table in rope_constants(length))
    hbm = pl.BlockSpec(memory_space=pltpu.HBM)
    vmem = pltpu.VMEM
    n_copies = 112
    act, dgrad = pl.pallas_call(
        kernel,
        out_shape=[jax.ShapeDtypeStruct((rows, width), BF16)] * 2,
        in_specs=[hbm] * 3 + [pl.BlockSpec(memory_space=pltpu.VMEM)] + [hbm] * 6,
        out_specs=[pl.BlockSpec(memory_space=pltpu.VMEM)] * 2,
        scratch_shapes=[vmem((rows, width), F32)] * 3
        + [vmem((width, feats), BF16)] * 5
        + [vmem((length, HD), F32)] * 2
        + [vmem((3 * feats, width), BF16), vmem((2 * feats, width), BF16)]
        + [vmem((length, width), BF16)] * 2
        + [vmem((length // 2, width), BF16)]
        + [vmem((length, feats), BF16)] * 4
        + [vmem((feats, length), BF16)] * 2
        + [vmem((length, HD), F32)] * 2
        + [vmem((length, 3 * feats), BF16), vmem((length, feats), BF16)]
        + [vmem((length // 2, feats), BF16)] * 2
        + [vmem((length, width), BF16), vmem((length // 2, width), BF16)]
        + [vmem((rows * 7, width), BF16), vmem((rows * 3, width), BF16)]
        + [vmem((rows, width), BF16)] * 2
        + [
            pltpu.SemaphoreType.DMA((9,)),
            pltpu.SemaphoreType.DMA((n_copies,)),
            pltpu.SemaphoreType.DMA((n_copies,)),
        ],
        compiler_params=pltpu.CompilerParams(
            collective_id=0, has_side_effects=True, vmem_limit_bytes=55_312_384
        ),
        name="relay_attention",
    )(
        x_fwd[0],
        x_bwd[0],
        grad_in[0],
        gain,
        w_query[0],
        w_key[0],
        w_value[0],
        w_out[0],
        cosine,
        sine,
    )
    return (act.astype(F32)[None], dgrad.astype(F32)[None])


def solution(mesh):
    placed = (
        P("pipe", "seq", None),
        P("pipe", "seq", None),
        P("pipe", "seq", None),
        P("pipe", None),
        P("pipe", None, "seq"),
        P("pipe", None, "seq"),
        P("pipe", None, "seq"),
        P("pipe", None, "seq"),
    )
    return jax.shard_map(
        shards,
        mesh=mesh,
        in_specs=placed,
        out_specs=(P("pipe", "seq", None), P("pipe", "seq", None)),
        check_vma=False,
    )
```
